128 devices in a mesh: req: 16 (over y, z), page: 8 (over x, core).
Axes of the slice: x: 4, y: 4, z: 4, core: 2. Of those that a mesh axis runs over, the one named last changes fastest.
Arguments:
- kv_store: bfloat16 [8192, 2, 8, 2048], P(('req', 'page')), may hold values from -6 to 6
- local_kv: bfloat16 [512, 2, 256, 2048], P(('req', 'page')), may hold values from -6 to 6
- new_qkv: bfloat16 [4, 512, 3, 2048], P(None, ('req', 'page')), may hold values from -32 to 32
- page_owner: int32 [512, 32], P(('req', 'page')), may hold values from 0 to 127, all different within a row; in each aligned block of 4 rows (0 to 3, 4 to 7, ...) at most 2 rows name the same one
- page_slot: int32 [512, 32], P(('req', 'page')), may hold values from 0 to 63
- prefix_len: int32 [512], P(('req', 'page')), may hold values from 225 to 256
- prefix_states: bfloat16 [16, 64, 64, 128], P('page'), may hold values from -6 to 6
- branch_id: int32 [512], P('req'), may hold values from 0 to 15
- mamba_x: bfloat16 [4, 512, 4096], P(None, ('req', 'page')), may hold values from -6 to 6
- mamba_bc: bfloat16 [4, 512, 256], P(None, ('req', 'page')), may hold values from -1.5 to 1.5
- mamba_dt: bfloat16 [4, 512, 64], P(None, ('req', 'page')), may hold values from -4 to 4
- decay_rate: float32 [64], replicated, may hold values from 0.05 to 4
Outputs:
- attn_out: bfloat16 [4, 512, 2048], P(None, ('req', 'page'))
- mamba_out: bfloat16 [4, 512, 4096], P(None, ('req', 'page'))
The draws below stay inside these ranges and needn't reach their ends.
Inputs may be any that keep to these rules, and one draw needn't show every extreme that they name: `page_owner`: A request's 32 pages lie on different devices; among the 4 requests of one device (aligned blocks of rows) no device is named more than 2 times, and one is named exactly 2 times.
All inputs are finite; a program needn't handle non-finite values.
Results may differ from the reference program's by a relative error of at most 0.0049.
Values may be sent and summed in bfloat16 or wider, within the bound.
No kernel may reach another device: no remote copies, remote signals or barrier semaphores. Data moves between devices by JAX's collectives and lax.ppermute only.
A program may use at most 192 MiB of HBM per device.

```python
import math
import jax
import jax.numpy as jnp
import numpy as np
from jax import lax

HEADS = 16
HEAD_DIM = 128
MAMBA_HEADS = 64
MAMBA_DIM = 64
STATE = 128
PAGE_TOK = 8
P_REQ = 32
STEPS = 4
R_DEV = 4
LOCAL_TOK = 256
PG_DEV = 64
CAP = 2
R = 512
NPAGES = 8192
NB = 16
DEVICES = 128


def draw_local_kv(key, part):
    full_shape = (R, 2, LOCAL_TOK, HEADS * HEAD_DIM)
    own_key = jax.random.fold_in(key, 11)
    values = jax.random.truncated_normal(own_key, -6.0, 6.0, full_shape, jnp.float32)
    return values.astype(jnp.bfloat16)


def draw_new_qkv(key, part):
    full_shape = (STEPS, R, 3, HEADS * HEAD_DIM)
    own_key = jax.random.fold_in(key, 23)
    values = jax.random.truncated_normal(own_key, -6.0, 6.0, full_shape, jnp.float32)
    return values.astype(jnp.bfloat16)


def with_ends(values, rng, low, largest):
    shape = values.shape
    index_at = [jax.random.randint(jax.random.fold_in(rng, axis), (), 0, shape[axis]) for axis in range(len(shape))]
    values = values.at[tuple(index_at)].set(low)
    longest = shape.index(max(shape))
    index_at[longest] = (index_at[longest] + 1) % shape[longest]
    return values.at[tuple(index_at)].set(largest)


def shard_levels(key, dims, pieces, low, largest):
    def one(dim, parts):
        steps = jax.random.uniform(jax.random.fold_in(jax.random.fold_in(key, 6), dim), (parts,), jnp.float32, low / len(pieces), largest / len(pieces))
        return jnp.repeat(jnp.exp(steps), dims[dim] // parts).reshape((-1,) + (1,) * (len(dims) - dim - 1))

    loudness = one(*pieces[0])
    for cut in pieces[1:]:
        loudness = loudness * one(*cut)
    return loudness


def cumulative_ranks(count, slope):
    portions = [(1 << 20) // math.isqrt(rank ** slope) + 1 for rank in range(1, count + 1)]
    width = 1 + sum(portions) // (1 << 30)
    return np.cumsum(np.array([max(1, weight // width) for weight in portions]))


def ranked_ids(key, extent, amount, slope):
    listing = cumulative_ranks(amount, slope)
    ticket = jax.random.randint(jax.random.fold_in(key, 1), extent, 0, int(listing[amount - 1]))
    standing = jnp.searchsorted(jnp.asarray(listing, jnp.int32), ticket, side="right")
    return jax.random.permutation(jax.random.fold_in(key, 2), amount)[standing].astype(jnp.int32)


def routed_block(rng, own, number, rows, count, top, bound, slope):
    order = jax.random.permutation(rng, count)
    packed, common = shares(count, rows * top, bound, slope, True), shares(count, rows * top, bound, slope, False)
    places = jnp.arange(count)

    def named(tallies, turn):
        used = int((tallies > 0).sum())
        fixed = max(1, used // 4)
        shifted = fixed + (places - fixed + turn * (used - fixed)) % max(1, count - fixed)
        return jnp.zeros((count,), jnp.int32).at[order[jnp.where(places < fixed, places, shifted)]].set(jnp.asarray(tallies, jnp.int32))

    tallies = jnp.where(number % 4 == 0, named(packed, number // 4), named(common, number - number // 4 - 1))
    mixed = jax.random.permutation(jax.random.fold_in(own, 3), count)
    giver, taker = mixed[0:count // 2 * 2:2], mixed[1:count // 2 * 2:2]
    room = jnp.minimum(tallies[giver] - 1, bound - tallies[taker]) // 2
    room = jnp.where((giver == order[0]) | (taker == order[0]) | (tallies[taker] == 0), 0, jnp.maximum(room, 0))
    shifted = jax.random.randint(jax.random.fold_in(own, 4), (count // 2,), 0, 1 << 20) % (room + 1)
    tallies = tallies.at[giver].add(-shifted).at[taker].add(shifted)
    labels = jnp.searchsorted(jnp.cumsum(tallies), jnp.arange(rows * top), side="right").astype(jnp.int32)
    listing = labels.reshape(top, rows).T
    listing = listing[jax.random.permutation(jax.random.fold_in(own, 1), rows)]
    turn = jax.random.randint(jax.random.fold_in(own, 2), (rows, 1), 0, top)
    return jnp.take_along_axis(listing, (jnp.arange(top)[None, :] + turn) % top, axis=1)


def shares(amount, total, bound, skew, full):
    portions = [(1 << 20) // math.isqrt(standing ** skew) + 1 for standing in range(1, amount + 1)]
    largest = bound if full else min(bound, max(-(-total // amount), total * portions[0] // sum(portions)))
    least = 1 if total - largest >= amount - 1 else 0
    counts, rest = [largest] + [least] * (amount - 1), total - largest - least * (amount - 1)
    while rest > 0:
        free = [i for i in range(1, amount) if counts[i] < largest] or [i for i in range(1, amount) if counts[i] < bound]
        mass, remaining = sum([portions[i] for i in free]), rest
        for i in free:
            addition = min(bound - counts[i], max(1, remaining * portions[i] // mass), rest)
            counts[i] = counts[i] + addition
            rest = rest - addition
    return np.array(counts)


def bell_draw(rng, dims, width, bound, cuts=(), held_as=jnp.bfloat16):
    gain = shard_levels(rng, dims, cuts, -0.22, 0.18) if cuts else 1.0
    result = jax.random.normal(rng, dims, jnp.float32) * width * gain
    return jnp.minimum(jnp.maximum(result, -bound), bound).astype(held_as)


def setup_inputs(seed: int = 0) -> dict:
    arg_keys = jax.random.split(jax.random.key(seed), 13)
    kv_store = bell_draw(arg_keys[0], (NPAGES, 2, PAGE_TOK, HEADS * HEAD_DIM), 1.0, 6.0, ((0, 128),))
    local_kv = draw_local_kv(jax.random.fold_in(arg_keys[12], 71), 0)
    new_qkv = draw_new_qkv(jax.random.fold_in(arg_keys[12], 71), 0)
    page_owner_keys = jax.random.split(jax.random.fold_in(arg_keys[3], 1), R // R_DEV)
    page_owner_turns = jax.random.permutation(jax.random.fold_in(arg_keys[3], 3), R // R_DEV)
    page_owner = jax.vmap(lambda own, number: routed_block(jax.random.fold_in(arg_keys[3], 2), own, number, R_DEV, DEVICES, P_REQ, CAP, 2))(page_owner_keys, page_owner_turns).reshape((R, P_REQ))
    page_slot = with_ends(jax.random.randint(arg_keys[4], (R, P_REQ), 0, PG_DEV), jax.random.fold_in(arg_keys[4], 1), 0, PG_DEV - 1).astype(jnp.int32)
    prefix_len = with_ends(jax.random.randint(arg_keys[5], (R,), (P_REQ - 4) * PAGE_TOK + 1, P_REQ * PAGE_TOK + 1), jax.random.fold_in(arg_keys[5], 1), (P_REQ - 4) * PAGE_TOK + 1, P_REQ * PAGE_TOK).astype(jnp.int32)
    prefix_states = bell_draw(arg_keys[6], (NB, MAMBA_HEADS, MAMBA_DIM, STATE), 1.0, 6.0, ((0, 8),))
    branch_id = with_ends(ranked_ids(arg_keys[7], (R,), NB, 2), jax.random.fold_in(arg_keys[7], 3), 0, NB - 1).astype(jnp.int32)
    mamba_x = bell_draw(arg_keys[8], (STEPS, R, MAMBA_HEADS * MAMBA_DIM), 1.0, 6.0, ((1, 128),))
    mamba_bc = bell_draw(arg_keys[9], (STEPS, R, 2 * STATE), 0.25, 1.5, ((1, 128),))
    mamba_dt = bell_draw(arg_keys[10], (STEPS, R, MAMBA_HEADS), 1.0, 4.0, ((1, 128),))
    decay_rate = jnp.clip(jnp.exp(jax.random.uniform(arg_keys[11], (MAMBA_HEADS,), jnp.float32, math.log(0.05), math.log(4.0))), 0.05, 4.0)
    return dict(kv_store=kv_store, local_kv=local_kv, new_qkv=new_qkv, page_owner=page_owner, page_slot=page_slot, prefix_len=prefix_len, prefix_states=prefix_states, branch_id=branch_id, mamba_x=mamba_x, mamba_bc=mamba_bc, mamba_dt=mamba_dt, decay_rate=decay_rate)


def split_heads(matrix, head_count):
    return matrix.reshape(matrix.shape[0], head_count, -1).astype(jnp.float32)

def attend(queries, page_keys, page_values, local_keys, local_values, new_keys, new_values, prefix_count):
    step_count = queries.shape[0]
    page_total = page_keys.shape[0]
    local_total = local_keys.shape[0]
    all_keys = jnp.concatenate([page_keys, local_keys, new_keys], axis=0)
    all_values = jnp.concatenate([page_values, local_values, new_values], axis=0)
    scores = jnp.einsum('shd,khd->hsk', split_heads(queries, HEADS), split_heads(all_keys, HEADS))
    scores = scores * (1.0 / math.sqrt(HEAD_DIM))
    key_index = jnp.arange(page_total + local_total + step_count, dtype=jnp.int32)
    new_index = key_index - page_total - local_total
    step_index = jnp.arange(step_count, dtype=jnp.int32)
    valid = (key_index[None, :] < prefix_count) | (key_index[None, :] >= page_total) & (new_index[None, :] <= step_index[:, None])
    scores = jnp.where(valid[None], scores, -jnp.inf)
    row_max = lax.optimization_barrier(jnp.max(scores, axis=-1, keepdims=True))
    exp_scores = jnp.exp(scores - row_max)
    weights = (exp_scores / lax.optimization_barrier(jnp.sum(exp_scores, axis=-1, keepdims=True))).astype(jnp.bfloat16)
    mixed = jnp.einsum('hsk,khd->shd', weights.astype(jnp.float32), split_heads(all_values, HEADS))
    return mixed.reshape(step_count, -1).astype(jnp.bfloat16)

def ssm_step(ssm_state, step_input, bc_input, dt_input, decay_rate):
    slot_count, head_count, head_width, state_width = ssm_state.shape
    step_delta = jax.nn.softplus(dt_input.astype(jnp.float32))
    decay = jnp.exp(-decay_rate[None, :] * step_delta)
    scaled_input = step_input.astype(jnp.float32).reshape(slot_count, head_count, head_width) * step_delta[:, :, None]
    bc_float = bc_input.astype(jnp.float32)
    b_vector = bc_float[:, :state_width]
    c_vector = bc_float[:, state_width:]
    ssm_state = decay[:, :, None, None] * ssm_state + scaled_input[:, :, :, None] * b_vector[:, None, None, :]
    output_row = lax.optimization_barrier(jnp.sum(ssm_state * c_vector[:, None, None, :], axis=-1))
    return (ssm_state, output_row.reshape(slot_count, -1).astype(jnp.bfloat16))

def reference(kv_store, local_kv, new_qkv, page_owner, page_slot, prefix_len, prefix_states, branch_id, mamba_x, mamba_bc, mamba_dt, decay_rate):
    features = kv_store.shape[-1]

    def one_request(request):
        store_rows = page_owner[request] * PG_DEV + page_slot[request]
        page_blocks = kv_store[store_rows]
        page_keys = page_blocks[:, 0].reshape(-1, features)
        page_values = page_blocks[:, 1].reshape(-1, features)
        return attend(new_qkv[:, request, 0], page_keys, page_values, local_kv[request, 0], local_kv[request, 1], new_qkv[:, request, 1], new_qkv[:, request, 2], prefix_len[request])
    attn_rows = lax.map(one_request, jnp.arange(R, dtype=jnp.int32))
    attn_out = jnp.transpose(attn_rows, (1, 0, 2))

    def one_scan(request):
        ssm_state = prefix_states[branch_id[request]].astype(jnp.float32)[None]
        outputs = []
        for step_index in range(STEPS):
            ssm_state, output_row = ssm_step(ssm_state, mamba_x[step_index, request][None], mamba_bc[step_index, request][None], mamba_dt[step_index, request][None], decay_rate)
            outputs.append(output_row[0])
        return jnp.stack(outputs)
    scan_rows = lax.map(one_scan, jnp.arange(R, dtype=jnp.int32))
    mamba_out = jnp.transpose(scan_rows, (1, 0, 2))
    return (attn_out, mamba_out)
```

```python
import functools
import math

import jax
import jax.numpy as jnp
from jax import lax
from jax.experimental import pallas as pl
from jax.experimental.pallas import tpu as pltpu
from jax.sharding import PartitionSpec as P

HEADS = 16
HD = 128
STEPS = 4
RD = 4
ROWS = STEPS * RD
FEAT = HEADS * HD
DEV = 128
TOK = 8
MH = 64
MD = 64
ST = 128
MF = MH * MD
NPG = 8
BATCH = 8
NB = DEV // BATCH
BLK = FEAT + 128
NEG = -1e30
SCALE = 1.0 / math.sqrt(HD)
BF = jnp.bfloat16
F32 = jnp.float32
NT = (((1,), (1,)), ((), ()))
NN = (((1,), (0,)), ((), ()))


def dot(a, b, dims=NN):
    return lax.dot_general(a, b, dims, preferred_element_type=F32)


def split2(x):
    hi = x.astype(BF)
    return hi, (x - hi.astype(F32)).astype(BF)


def split3(x):
    hi = x.astype(BF)
    rest = x - hi.astype(F32)
    mid = rest.astype(BF)
    return hi, mid, (rest - mid.astype(F32)).astype(BF)


def local_kernel(q_ref, nk_ref, nv_ref, kv_ref, o_ref, m_ref, l_ref):
    q = q_ref[...]
    parts = [dot(q, kv_ref[r, 0], NT) for r in range(RD)]
    row = lax.broadcasted_iota(jnp.int32, (ROWS, 1), 0)
    keep = row % RD
    new = dot(q, nk_ref[...], NT) * SCALE
    col = lax.broadcasted_iota(jnp.int32, (ROWS, ROWS), 1)
    ok = (col % RD == keep) & (col // RD <= row // RD)
    new = jnp.where(ok, new, NEG)
    mine = jnp.where(keep == 0, parts[0], NEG)
    for r in range(1, RD):
        mine = jnp.where(keep == r, parts[r], mine)
    mine = mine * SCALE
    top = jnp.maximum(jnp.max(mine, axis=1, keepdims=True), jnp.max(new, axis=1, keepdims=True))
    p = jnp.exp(mine - top)
    pn = jnp.where(ok, jnp.exp(new - top), 0.0)
    total = jnp.sum(p, axis=1, keepdims=True) + jnp.sum(pn, axis=1, keepdims=True)
    out = dot(pn.astype(BF), nv_ref[...])
    for r in range(RD):
        out = out + dot(jnp.where(keep == r, p, 0.0).astype(BF), kv_ref[r, 1])
    o_ref[...] = out
    m_ref[...] = jnp.broadcast_to(top, (ROWS, HD))
    l_ref[...] = jnp.broadcast_to(total, (ROWS, HD))


def local_attention(q, nk, nv, local_kv):
    row = pl.BlockSpec((ROWS, HD), lambda h: (0, h))
    return pl.pallas_call(
        local_kernel,
        grid=(HEADS,),
        in_specs=[row, row, row, pl.BlockSpec((RD, 2, 256, HD), lambda h: (0, 0, 0, h))],
        out_specs=[row, row, row],
        out_shape=[jax.ShapeDtypeStruct((ROWS, FEAT), F32)] * 3,
        cost_estimate=pl.CostEstimate(flops=2 * 2 * 16 * 1024 * 2048, bytes_accessed=9_000_000, transcendentals=300_000),
        name="local_attention",
    )(q, nk, nv, local_kv)


def owner_kernel(slot_ref, kreq_ref, sel_ref, q_ref, kv_ref, o_ref, kbuf, vbuf, sem):
    step = pl.program_id(0)
    pages = 2 * BATCH

    def copies(at, buf):
        out = []
        for j in range(pages):
            page = slot_ref[at * pages + j]
            out.append(pltpu.make_async_copy(kv_ref.at[page, 0], kbuf.at[buf, j], sem.at[buf, 0, j]))
            out.append(pltpu.make_async_copy(kv_ref.at[page, 1], vbuf.at[buf, j], sem.at[buf, 1, j]))
        return out

    @pl.when(step == 0)
    def _():
        for c in copies(0, 0):
            c.start()

    now = lax.rem(step, 2)

    @pl.when(step + 1 < NB)
    def _():
        for c in copies(step + 1, 1 - now):
            c.start()

    for c in copies(step, now):
        c.wait()
    rows = BATCH * ROWS
    keys = pages * TOK
    row = lax.broadcasted_iota(jnp.int32, (rows, 1), 0)
    mine = (row // ROWS) * RD + row % RD
    ok = mine == kreq_ref[0]
    lane = lax.broadcasted_iota(jnp.int32, (rows, HD), 1)
    tops = jnp.zeros((rows, HD), F32)
    sums = jnp.zeros((rows, HD), F32)
    sel = sel_ref[...]
    for h in range(HEADS):
        at = slice(h * HD, (h + 1) * HD)
        q = q_ref[:, :, at].reshape(rows, HD)
        k = kbuf[now, :, :, at].reshape(keys, HD)
        v = vbuf[now, :, :, at].reshape(keys, HD)
        s = jnp.where(ok, dot(q, k, NT) * SCALE, NEG)
        top = jnp.max(s, axis=1, keepdims=True)
        p = jnp.where(ok, jnp.exp(s - top), 0.0)
        tops = jnp.where(lane == h, top, tops)
        sums = jnp.where(lane == h, jnp.sum(p, axis=1, keepdims=True), sums)
        out = dot(p.astype(BF), v).astype(BF)
        o_ref[:, at] = dot(sel, out).astype(BF)
    parts = list(split3(tops)) + list(split2(sums))
    stats = jnp.zeros((rows, HD), F32)
    for i, part in enumerate(parts):
        wide = part.astype(F32)
        if i:
            wide = pltpu.roll(wide, HEADS * i, 1)
        stats = stats + wide
    o_ref[:, FEAT:] = dot(sel, stats.astype(BF)).astype(BF)


def owner_attention(slots, kreq, sel, gathered, kv_store):
    rows = BATCH * 2 * STEPS
    return pl.pallas_call(
        owner_kernel,
        grid_spec=pltpu.PrefetchScalarGridSpec(
            num_scalar_prefetch=1,
            grid=(NB,),
            in_specs=[
                pl.BlockSpec((1, 1, 2 * BATCH * TOK), lambda i, s: (i, 0, 0)),
                pl.BlockSpec((rows, BATCH * ROWS), lambda i, s: (i, 0)),
                pl.BlockSpec((BATCH, ROWS, BLK), lambda i, s: (i, 0, 0)),
                pl.BlockSpec(memory_space=pl.ANY),
            ],
            out_specs=pl.BlockSpec((rows, BLK), lambda i, s: (i, 0)),
            scratch_shapes=[
                pltpu.VMEM((2, 2 * BATCH, TOK, FEAT), BF),
                pltpu.VMEM((2, 2 * BATCH, TOK, FEAT), BF),
                pltpu.SemaphoreType.DMA((2, 2, 2 * BATCH)),
            ],
        ),
        out_shape=jax.ShapeDtypeStruct((DEV * 2 * STEPS, BLK), BF),
        cost_estimate=pl.CostEstimate(flops=4 * 2048 * 128 * 2048, bytes_accessed=30_000_000, transcendentals=4_000_000),
        compiler_params=pltpu.CompilerParams(vmem_limit_bytes=32 * 1024 * 1024),
        name="owner_attention",
    )(slots, kreq, sel, gathered, kv_store)


def combine_kernel(own_ref, got_ref, o_ref, m_ref, l_ref, out_ref):
    cols = DEV * 2 * STEPS
    own = own_ref[...]
    row = lax.broadcasted_iota(jnp.int32, (ROWS, 1), 0)
    ok = row == own
    stats = jnp.transpose(got_ref[:, FEAT:].astype(F32))
    part = [stats[HEADS * i : HEADS * (i + 1)] for i in range(5)]
    tops = part[0] + part[1] + part[2]
    sums = part[3] + part[4]
    for h in range(HEADS):
        at = slice(h * HD, (h + 1) * HD)
        top = jnp.where(ok, tops[h : h + 1], NEG)
        lm = m_ref[:, h * HD : h * HD + 1]
        best = jnp.maximum(jnp.max(top, axis=1, keepdims=True), lm)
        w = jnp.where(ok, jnp.exp(top - best), 0.0)
        mine = jnp.exp(lm - best)
        total = jnp.sum(w * sums[h : h + 1], axis=1, keepdims=True) + mine * l_ref[:, h * HD : h * HD + 1]
        hi, lo = split2(w)
        got = got_ref[:, at]
        mix = dot(hi, got) + dot(lo, got) + mine * o_ref[:, at]
        out_ref[:, at] = (mix / total).astype(BF)


def combine(own, got, o, m, l):
    return pl.pallas_call(
        combine_kernel,
        out_shape=jax.ShapeDtypeStruct((ROWS, FEAT), BF),
        compiler_params=pltpu.CompilerParams(vmem_limit_bytes=32 * 1024 * 1024),
        cost_estimate=pl.CostEstimate(flops=4 * 16 * 1024 * 2048, bytes_accessed=5_000_000, transcendentals=300_000),
        name="combine_attention",
    )(own, got, o, m, l)


def state_kernel(br_ref, c_ref, st_ref, *outs):
    c = c_ref[...]
    first = dot(c, st_ref[0], NT)
    second = dot(c, st_ref[1], NT)
    which = br_ref[...]
    z = jnp.where(which == 0, first, 0.0) + jnp.where(which == 1, second, 0.0)
    z = z.astype(BF)
    for k in range(NPG):
        outs[k][...] = z[k * ROWS : (k + 1) * ROWS]


def state_products(which, c_all, states):
    wide = 1024
    return pl.pallas_call(
        state_kernel,
        grid=(MF // wide,),
        in_specs=[
            pl.BlockSpec((NPG * ROWS, 1), lambda i: (0, 0)),
            pl.BlockSpec((NPG * ROWS, ST), lambda i: (0, 0)),
            pl.BlockSpec((2, wide, ST), lambda i: (0, i, 0)),
        ],
        out_specs=[pl.BlockSpec((ROWS, wide), lambda i: (0, i))] * NPG,
        out_shape=[jax.ShapeDtypeStruct((ROWS, MF), BF)] * NPG,
        cost_estimate=pl.CostEstimate(flops=4 * 128 * 128 * 4096, bytes_accessed=3_200_000, transcendentals=0),
        name="state_products",
    )(which, c_all, states)


def scan_kernel(coef_ref, x_ref, *refs):
    zs, out_ref = refs[:-1], refs[-1]
    wide = out_ref.shape[1]
    head = lax.broadcasted_iota(jnp.int32, (MH, wide), 0)
    chan = lax.broadcasted_iota(jnp.int32, (MH, wide), 1) + pl.program_id(0) * wide
    spread = (head == chan // MD).astype(BF)
    hi, mid, lo = split3(coef_ref[...])
    coef = dot(hi, spread) + dot(mid, spread) + dot(lo, spread)
    z = zs[0][...].astype(F32)
    for ref in zs[1:]:
        z = z + ref[...].astype(F32)
    y = coef[:ROWS] * z
    x = x_ref[...].astype(F32)
    for t in range(STEPS):
        xt = jnp.concatenate([x[t * RD : (t + 1) * RD]] * STEPS, axis=0)
        y = y + coef[(t + 1) * ROWS : (t + 2) * ROWS] * xt
    out_ref[...] = y.astype(BF)


def scan_outputs(coef, x, zs):
    wide = 1024
    spec = pl.BlockSpec((ROWS, wide), lambda i: (0, i))
    return pl.pallas_call(
        scan_kernel,
        grid=(MF // wide,),
        in_specs=[pl.BlockSpec(coef.shape, lambda i: (0, 0))] + [spec] * (1 + NPG),
        out_specs=spec,
        out_shape=jax.ShapeDtypeStruct((ROWS, MF), BF),
        cost_estimate=pl.CostEstimate(flops=6 * 80 * 64 * 4096, bytes_accessed=1_500_000, transcendentals=0),
        name="scan_outputs",
    )(coef, x, *zs)


def coefficients(mamba_bc, mamba_dt, decay_rate):
    delta = jax.nn.softplus(mamba_dt.astype(F32))
    rate = -decay_rate[None, :] * delta
    decay = jnp.exp(rate)
    b, c = mamba_bc[:, :, :ST], mamba_bc[:, :, ST:]
    bc = jnp.einsum("trn,srn->tsr", b, c, preferred_element_type=F32)
    rows = []
    run = decay[0]
    for s in range(STEPS):
        rows.append(run)
        if s + 1 < STEPS:
            run = run * decay[s + 1]
    zero = jnp.zeros_like(run)
    for t in range(STEPS):
        carry = delta[t]
        for s in range(STEPS):
            if s < t:
                rows.append(zero)
                continue
            if s > t:
                carry = carry * decay[s]
            rows.append(carry * bc[t, s][:, None])
    return jnp.stack(rows).reshape((1 + STEPS) * ROWS, MH)


def on_device(
    kv_store,
    local_kv,
    new_qkv,
    page_owner,
    page_slot,
    prefix_len,
    prefix_states,
    branch_id,
    mamba_x,
    mamba_bc,
    mamba_dt,
    decay_rate,
):
    me = lax.axis_index(("req", "page"))
    my_page = lax.axis_index("page")
    q = new_qkv[:, :, 0].reshape(ROWS, FEAT)
    nk = new_qkv[:, :, 1].reshape(ROWS, FEAT)
    nv = new_qkv[:, :, 2].reshape(ROWS, FEAT)

    count = jnp.clip(prefix_len[:, None] - TOK * jnp.arange(page_owner.shape[1], dtype=jnp.int32)[None, :], 0, TOK)
    named = page_owner[:, :, None] == jnp.arange(DEV, dtype=jnp.int32)[None, None, :]
    t_slot = jnp.sum(jnp.where(named, page_slot[:, :, None], 0), axis=1)
    t_count = jnp.sum(jnp.where(named, count[:, :, None], 0), axis=1)
    tables = jnp.concatenate([t_slot, t_count, jnp.zeros((2 * RD, DEV), jnp.int32)], axis=0).astype(BF)
    block = jnp.concatenate([q, tables], axis=1)
    gathered = lax.all_gather(block[None], ("req", "page"), axis=0, tiled=True)

    c_own = mamba_bc[:, :, ST:].reshape(ROWS, ST)
    c_rel = [c_own]
    for k in range(1, NPG):
        c_rel.append(lax.ppermute(c_own, "page", [((i + k) % NPG, i) for i in range(NPG)]))
    order = (my_page + jnp.arange(NPG, dtype=jnp.int32)) % NPG
    branch = branch_id.reshape(NPG, RD)[order] - 2 * my_page
    branch = jnp.broadcast_to(branch[:, None, :], (NPG, STEPS, RD)).reshape(NPG * ROWS, 1)
    z_out = state_products(branch, jnp.concatenate(c_rel, axis=0), prefix_states.reshape(2, MF, ST))
    z_in = [z_out[0]]
    for k in range(1, NPG):
        z_in.append(lax.ppermute(z_out[k], "page", [(i, (i + k) % NPG) for i in range(NPG)]))
    coef = coefficients(mamba_bc, mamba_dt, decay_rate)
    mamba_out = scan_outputs(coef, mamba_x.reshape(ROWS, MF), z_in)

    o, m, l = local_attention(q, nk, nv, local_kv)

    mine = (jnp.arange(DEV, dtype=jnp.int32) == me).astype(BF)
    col = jnp.einsum("drl,l->rd", gathered[:, : 2 * RD, FEAT:], mine, preferred_element_type=F32).astype(jnp.int32)
    c_slot, c_count = col[:RD], col[RD:]
    hit = (c_count > 0).astype(jnp.int32)
    rank = jnp.cumsum(hit, axis=0) - hit
    request = jnp.arange(RD, dtype=jnp.int32)[:, None]
    at_slot, at_req, at_count = [], [], []
    for c in range(2):
        here = (hit > 0) & (rank == c)
        at_slot.append(jnp.sum(jnp.where(here, c_slot, 0), axis=0))
        at_count.append(jnp.sum(jnp.where(here, c_count, 0), axis=0))
        at_req.append(jnp.sum(jnp.where(here, request + 1, 0), axis=0) - 1)
    at_slot = jnp.stack(at_slot, axis=1)
    at_count = jnp.stack(at_count, axis=1)
    at_req = jnp.stack(at_req, axis=1)
    near = jnp.arange(DEV, dtype=jnp.int32)[:, None] % BATCH
    full = jnp.where(at_count > 0, near * RD + at_req, -1)
    tok = jnp.arange(TOK, dtype=jnp.int32)
    kreq = jnp.where(tok[None, None, :] < at_count[:, :, None], full[:, :, None], -1).reshape(NB, 1, 2 * BATCH * TOK)
    lane = jnp.arange(BATCH * ROWS, dtype=jnp.int32)
    lane_req = (lane // ROWS) * RD + lane % RD
    lane_step = (lane // RD) % STEPS
    steps = jnp.arange(STEPS, dtype=jnp.int32)
    sel = (full[:, :, None, None] == lane_req) & (steps[None, None, :, None] == lane_step)
    sel = sel.astype(BF).reshape(DEV * 2 * STEPS, BATCH * ROWS)
    part = owner_attention(at_slot.reshape(-1), kreq, sel, gathered, kv_store)
    got = lax.all_to_all(part.reshape(DEV, 2 * STEPS, BLK), ("req", "page"), 0, 0, tiled=True)

    own_hit = (t_count > 0).astype(jnp.int32)
    own_rank = jnp.cumsum(own_hit, axis=0) - own_hit
    places = []
    for c in range(2):
        here = (own_hit > 0) & (own_rank == c)
        places.append(jnp.sum(jnp.where(here, request + 1, 0), axis=0) - 1)
    places = jnp.stack(places, axis=1)[:, :, None]
    own = jnp.where(places >= 0, steps[None, None, :] * RD + places, -1).reshape(1, DEV * 2 * STEPS)
    attn = combine(own, got.reshape(DEV * 2 * STEPS, BLK), o, m, l)
    return attn.reshape(STEPS, RD, FEAT), mamba_out.reshape(STEPS, RD, MF)


def solution(mesh):
    in_specs = (
        P(("req", "page"), None, None, None),
        P(("req", "page"), None, None, None),
        P(None, ("req", "page"), None, None),
        P(("req", "page"), None),
        P(("req", "page"), None),
        P(("req", "page")),
        P("page", None, None, None),
        P("req"),
        P(None, ("req", "page"), None),
        P(None, ("req", "page"), None),
        P(None, ("req", "page"), None),
        P(),
    )
    out_specs = (P(None, ("req", "page"), None), P(None, ("req", "page"), None))
    return jax.shard_map(
        on_device, mesh=mesh, in_specs=in_specs, out_specs=out_specs, check_vma=False
    )
```

```python
import functools
import math

import jax
import jax.numpy as jnp
from jax import lax
from jax.experimental import pallas as pl
from jax.experimental.pallas import tpu as pltpu
from jax.sharding import PartitionSpec as P

HEADS = 16
HD = 128
STEPS = 4
RD = 4
ROWS = STEPS * RD
FEAT = HEADS * HD
DEV = 128
TOK = 8
MH = 64
MD = 64
ST = 128
MF = MH * MD
NPG = 8
BATCH = 16
NB = DEV // BATCH
JOBS = 2 * BATCH
LANES = JOBS * STEPS
BLK = FEAT + 128
NEG = -1e30
SCALE = 1.0 / math.sqrt(HD)
BF = jnp.bfloat16
F32 = jnp.float32
NT = (((1,), (1,)), ((), ()))
NN = (((1,), (0,)), ((), ()))


def dot(a, b, dims=NN):
    return lax.dot_general(a, b, dims, preferred_element_type=F32)


def split2(x):
    hi = x.astype(BF)
    return hi, (x - hi.astype(F32)).astype(BF)


def split3(x):
    hi = x.astype(BF)
    rest = x - hi.astype(F32)
    mid = rest.astype(BF)
    return hi, mid, (rest - mid.astype(F32)).astype(BF)


def local_kernel(q_ref, nk_ref, nv_ref, kv_ref, o_ref, m_ref, l_ref):
    q = q_ref[...]
    parts = [dot(q, kv_ref[r, 0], NT) for r in range(RD)]
    row = lax.broadcasted_iota(jnp.int32, (ROWS, 1), 0)
    keep = row % RD
    new = dot(q, nk_ref[...], NT) * SCALE
    col = lax.broadcasted_iota(jnp.int32, (ROWS, ROWS), 1)
    ok = (col % RD == keep) & (col // RD <= row // RD)
    new = jnp.where(ok, new, NEG)
    mine = jnp.where(keep == 0, parts[0], NEG)
    for r in range(1, RD):
        mine = jnp.where(keep == r, parts[r], mine)
    mine = mine * SCALE
    top = jnp.maximum(jnp.max(mine, axis=1, keepdims=True), jnp.max(new, axis=1, keepdims=True))
    p = jnp.exp(mine - top)
    pn = jnp.where(ok, jnp.exp(new - top), 0.0)
    total = jnp.sum(p, axis=1, keepdims=True) + jnp.sum(pn, axis=1, keepdims=True)
    out = dot(pn.astype(BF), nv_ref[...])
    for r in range(RD):
        out = out + dot(jnp.where(keep == r, p, 0.0).astype(BF), kv_ref[r, 1])
    o_ref[...] = out
    m_ref[...] = jnp.broadcast_to(top, (ROWS, HD))
    l_ref[...] = jnp.broadcast_to(total, (ROWS, HD))


def local_attention(q, nk, nv, local_kv):
    row = pl.BlockSpec((ROWS, HD), lambda h: (0, h))
    return pl.pallas_call(
        local_kernel,
        grid=(HEADS,),
        in_specs=[row, row, row, pl.BlockSpec((RD, 2, 256, HD), lambda h: (0, 0, 0, h))],
        out_specs=[row, row, row],
        out_shape=[jax.ShapeDtypeStruct((ROWS, FEAT), F32)] * 3,
        cost_estimate=pl.CostEstimate(flops=2 * 2 * 16 * 1024 * 2048, bytes_accessed=9_000_000, transcendentals=300_000),
        name="local_attention",
    )(q, nk, nv, local_kv)


def owner_kernel(slot_ref, cnt_ref, sel_ref, tile_ref, q_ref, kv_ref, o_ref, kbuf, vbuf, qbuf, sbuf, sem):
    step = pl.program_id(0)
    now = lax.rem(step, 2)

    def copies(at, buf):
        out = []
        for j in range(JOBS):
            page = slot_ref[at * JOBS + j]
            out.append(pltpu.make_async_copy(kv_ref.at[page, 0], kbuf.at[buf, j], sem.at[buf, 0, j]))
            out.append(pltpu.make_async_copy(kv_ref.at[page, 1], vbuf.at[buf, j], sem.at[buf, 1, j]))
        return out

    @pl.when(step == 0)
    def _():
        for c in copies(0, 0):
            c.start()

    @pl.when(step + 1 < NB)
    def _():
        for c in copies(step + 1, 1 - now):
            c.start()

    q = q_ref[:, :, :FEAT].reshape(BATCH * ROWS, FEAT)
    qbuf[...] = dot(sel_ref[...], q).astype(BF)
    for c in copies(step, now):
        c.wait()
    lane = lax.broadcasted_iota(jnp.int32, (JOBS, TOK, LANES), 2)
    job = lax.broadcasted_iota(jnp.int32, (JOBS, TOK, LANES), 0)
    here = job == lane // STEPS
    for h in range(HEADS):
        at = slice(h * HD, (h + 1) * HD)
        k = kbuf[now, :, :, at].reshape(JOBS * TOK, HD)
        s = dot(k, qbuf[:, at], NT).reshape(JOBS, TOK, LANES)
        sbuf[h] = jnp.sum(jnp.where(here, s, 0.0), axis=0)
    tok = lax.broadcasted_iota(jnp.int32, (HEADS, TOK, LANES), 1)
    ok = tok < cnt_ref[...]
    s = jnp.where(ok, sbuf[...] * SCALE, NEG)
    top = jnp.max(s, axis=1, keepdims=True)
    p = jnp.where(ok, jnp.exp(s - top), 0.0)
    total = jnp.sum(p, axis=1)
    top = jnp.max(s, axis=1)
    parts = [x.astype(F32) for x in list(split3(top)) + list(split2(total))]
    parts.append(jnp.zeros((HD - HEADS * len(parts), LANES), F32))
    o_ref[:, FEAT:] = jnp.transpose(jnp.concatenate(parts, axis=0)).astype(BF)
    pt = jnp.transpose(p.reshape(HEADS * TOK, LANES)).astype(BF)
    row = lax.broadcasted_iota(jnp.int32, (LANES, JOBS * TOK), 0)
    key = lax.broadcasted_iota(jnp.int32, (LANES, JOBS * TOK), 1)
    own = row // STEPS == key // TOK
    for h in range(HEADS):
        at = slice(h * HD, (h + 1) * HD)
        w = dot(pt, tile_ref[h])
        w = jnp.where(own, w, 0.0).astype(BF)
        v = vbuf[now, :, :, at].reshape(JOBS * TOK, HD)
        o_ref[:, at] = dot(w, v).astype(BF)


def owner_attention(slots, counts, sel, tile, gathered, kv_store):
    return pl.pallas_call(
        owner_kernel,
        grid_spec=pltpu.PrefetchScalarGridSpec(
            num_scalar_prefetch=1,
            grid=(NB,),
            in_specs=[
                pl.BlockSpec((1, 1, LANES), lambda i, s: (i, 0, 0)),
                pl.BlockSpec((LANES, BATCH * ROWS), lambda i, s: (i, 0)),
                pl.BlockSpec((HEADS, HEADS * TOK, JOBS * TOK), lambda i, s: (0, 0, 0)),
                pl.BlockSpec((BATCH, ROWS, BLK), lambda i, s: (i, 0, 0)),
                pl.BlockSpec(memory_space=pl.ANY),
            ],
            out_specs=pl.BlockSpec((LANES, BLK), lambda i, s: (i, 0)),
            scratch_shapes=[
                pltpu.VMEM((2, JOBS, TOK, FEAT), BF),
                pltpu.VMEM((2, JOBS, TOK, FEAT), BF),
                pltpu.VMEM((LANES, FEAT), BF),
                pltpu.VMEM((HEADS, TOK, LANES), F32),
                pltpu.SemaphoreType.DMA((2, 2, JOBS)),
            ],
        ),
        out_shape=jax.ShapeDtypeStruct((DEV * 2 * STEPS, BLK), BF),
        cost_estimate=pl.CostEstimate(flops=4 * 2048 * 128 * 2048, bytes_accessed=30_000_000, transcendentals=200_000),
        compiler_params=pltpu.CompilerParams(vmem_limit_bytes=32 * 1024 * 1024),
        name="owner_attention",
    )(slots, counts, sel, tile, gathered, kv_store)


def combine_kernel(own_ref, got_ref, o_ref, m_ref, l_ref, out_ref):
    cols = DEV * 2 * STEPS
    own = own_ref[...]
    row = lax.broadcasted_iota(jnp.int32, (ROWS, 1), 0)
    ok = row == own
    stats = jnp.transpose(got_ref[:, FEAT:].astype(F32))
    part = [stats[HEADS * i : HEADS * (i + 1)] for i in range(5)]
    tops = part[0] + part[1] + part[2]
    sums = part[3] + part[4]
    for h in range(HEADS):
        at = slice(h * HD, (h + 1) * HD)
        top = jnp.where(ok, tops[h : h + 1], NEG)
        lm = m_ref[:, h * HD : h * HD + 1]
        best = jnp.maximum(jnp.max(top, axis=1, keepdims=True), lm)
        w = jnp.where(ok, jnp.exp(top - best), 0.0)
        mine = jnp.exp(lm - best)
        total = jnp.sum(w * sums[h : h + 1], axis=1, keepdims=True) + mine * l_ref[:, h * HD : h * HD + 1]
        hi, lo = split2(w)
        got = got_ref[:, at]
        mix = dot(hi, got) + dot(lo, got) + mine * o_ref[:, at]
        out_ref[:, at] = (mix / total).astype(BF)


def combine(own, got, o, m, l):
    return pl.pallas_call(
        combine_kernel,
        out_shape=jax.ShapeDtypeStruct((ROWS, FEAT), BF),
        compiler_params=pltpu.CompilerParams(vmem_limit_bytes=32 * 1024 * 1024),
        cost_estimate=pl.CostEstimate(flops=4 * 16 * 1024 * 2048, bytes_accessed=5_000_000, transcendentals=300_000),
        name="combine_attention",
    )(own, got, o, m, l)


def state_kernel(br_ref, c_ref, st_ref, *outs):
    c = c_ref[...]
    first = dot(c, st_ref[0], NT)
    second = dot(c, st_ref[1], NT)
    which = br_ref[...]
    z = jnp.where(which == 0, first, 0.0) + jnp.where(which == 1, second, 0.0)
    z = z.astype(BF)
    for k in range(NPG):
        outs[k][...] = z[k * ROWS : (k + 1) * ROWS]


def state_products(which, c_all, states):
    wide = 1024
    return pl.pallas_call(
        state_kernel,
        grid=(MF // wide,),
        in_specs=[
            pl.BlockSpec((NPG * ROWS, 1), lambda i: (0, 0)),
            pl.BlockSpec((NPG * ROWS, ST), lambda i: (0, 0)),
            pl.BlockSpec((2, wide, ST), lambda i: (0, i, 0)),
        ],
        out_specs=[pl.BlockSpec((ROWS, wide), lambda i: (0, i))] * NPG,
        out_shape=[jax.ShapeDtypeStruct((ROWS, MF), BF)] * NPG,
        cost_estimate=pl.CostEstimate(flops=4 * 128 * 128 * 4096, bytes_accessed=3_200_000, transcendentals=0),
        name="state_products",
    )(which, c_all, states)


def scan_kernel(coef_ref, x_ref, *refs):
    zs, out_ref = refs[:-1], refs[-1]
    wide = out_ref.shape[1]
    head = lax.broadcasted_iota(jnp.int32, (MH, wide), 0)
    chan = lax.broadcasted_iota(jnp.int32, (MH, wide), 1) + pl.program_id(0) * wide
    spread = (head == chan // MD).astype(BF)
    hi, mid, lo = split3(coef_ref[...])
    coef = dot(hi, spread) + dot(mid, spread) + dot(lo, spread)
    z = zs[0][...].astype(F32)
    for ref in zs[1:]:
        z = z + ref[...].astype(F32)
    y = coef[:ROWS] * z
    x = x_ref[...].astype(F32)
    for t in range(STEPS):
        xt = jnp.concatenate([x[t * RD : (t + 1) * RD]] * STEPS, axis=0)
        y = y + coef[(t + 1) * ROWS : (t + 2) * ROWS] * xt
    out_ref[...] = y.astype(BF)


def scan_outputs(coef, x, zs):
    wide = 1024
    spec = pl.BlockSpec((ROWS, wide), lambda i: (0, i))
    return pl.pallas_call(
        scan_kernel,
        grid=(MF // wide,),
        in_specs=[pl.BlockSpec(coef.shape, lambda i: (0, 0))] + [spec] * (1 + NPG),
        out_specs=spec,
        out_shape=jax.ShapeDtypeStruct((ROWS, MF), BF),
        cost_estimate=pl.CostEstimate(flops=6 * 80 * 64 * 4096, bytes_accessed=1_500_000, transcendentals=0),
        name="scan_outputs",
    )(coef, x, *zs)


def coefficients(mamba_bc, mamba_dt, decay_rate):
    delta = jax.nn.softplus(mamba_dt.astype(F32))
    rate = -decay_rate[None, :] * delta
    decay = jnp.exp(rate)
    b, c = mamba_bc[:, :, :ST], mamba_bc[:, :, ST:]
    bc = jnp.einsum("trn,srn->tsr", b, c, preferred_element_type=F32)
    rows = []
    run = decay[0]
    for s in range(STEPS):
        rows.append(run)
        if s + 1 < STEPS:
            run = run * decay[s + 1]
    zero = jnp.zeros_like(run)
    for t in range(STEPS):
        carry = delta[t]
        for s in range(STEPS):
            if s < t:
                rows.append(zero)
                continue
            if s > t:
                carry = carry * decay[s]
            rows.append(carry * bc[t, s][:, None])
    return jnp.stack(rows).reshape((1 + STEPS) * ROWS, MH)


def on_device(
    kv_store,
    local_kv,
    new_qkv,
    page_owner,
    page_slot,
    prefix_len,
    prefix_states,
    branch_id,
    mamba_x,
    mamba_bc,
    mamba_dt,
    decay_rate,
):
    me = lax.axis_index(("req", "page"))
    my_page = lax.axis_index("page")
    q = new_qkv[:, :, 0].reshape(ROWS, FEAT)
    nk = new_qkv[:, :, 1].reshape(ROWS, FEAT)
    nv = new_qkv[:, :, 2].reshape(ROWS, FEAT)

    count = jnp.clip(prefix_len[:, None] - TOK * jnp.arange(page_owner.shape[1], dtype=jnp.int32)[None, :], 0, TOK)
    named = page_owner[:, :, None] == jnp.arange(DEV, dtype=jnp.int32)[None, None, :]
    t_slot = jnp.sum(jnp.where(named, page_slot[:, :, None], 0), axis=1)
    t_count = jnp.sum(jnp.where(named, count[:, :, None], 0), axis=1)
    tables = jnp.concatenate([t_slot, t_count, jnp.zeros((2 * RD, DEV), jnp.int32)], axis=0).astype(BF)
    block = jnp.concatenate([q, tables], axis=1)
    gathered = lax.all_gather(block[None], ("req", "page"), axis=0, tiled=True)

    c_own = mamba_bc[:, :, ST:].reshape(ROWS, ST)
    c_rel = [c_own]
    for k in range(1, NPG):
        c_rel.append(lax.ppermute(c_own, "page", [((i + k) % NPG, i) for i in range(NPG)]))
    order = (my_page + jnp.arange(NPG, dtype=jnp.int32)) % NPG
    branch = branch_id.reshape(NPG, RD)[order] - 2 * my_page
    branch = jnp.broadcast_to(branch[:, None, :], (NPG, STEPS, RD)).reshape(NPG * ROWS, 1)
    z_out = state_products(branch, jnp.concatenate(c_rel, axis=0), prefix_states.reshape(2, MF, ST))
    z_in = [z_out[0]]
    for k in range(1, NPG):
        z_in.append(lax.ppermute(z_out[k], "page", [(i, (i + k) % NPG) for i in range(NPG)]))
    coef = coefficients(mamba_bc, mamba_dt, decay_rate)
    mamba_out = scan_outputs(coef, mamba_x.reshape(ROWS, MF), z_in)

    o, m, l = local_attention(q, nk, nv, local_kv)

    gathered, o, m, l, mamba_out = lax.optimization_barrier((gathered, o, m, l, mamba_out))
    mine = (jnp.arange(DEV, dtype=jnp.int32) == me).astype(BF)
    col = jnp.einsum("drl,l->rd", gathered[:, : 2 * RD, FEAT:], mine, preferred_element_type=F32).astype(jnp.int32)
    c_slot, c_count = col[:RD], col[RD:]
    hit = (c_count > 0).astype(jnp.int32)
    rank = jnp.cumsum(hit, axis=0) - hit
    request = jnp.arange(RD, dtype=jnp.int32)[:, None]
    at_slot, at_req, at_count = [], [], []
    for c in range(2):
        here = (hit > 0) & (rank == c)
        at_slot.append(jnp.sum(jnp.where(here, c_slot, 0), axis=0))
        at_count.append(jnp.sum(jnp.where(here, c_count, 0), axis=0))
        at_req.append(jnp.sum(jnp.where(here, request + 1, 0), axis=0) - 1)
    at_slot = jnp.stack(at_slot, axis=1)
    at_count = jnp.stack(at_count, axis=1)
    at_req = jnp.stack(at_req, axis=1)
    near = jnp.arange(DEV, dtype=jnp.int32)[:, None] % BATCH
    full = jnp.where(at_count > 0, near * RD + at_req, -1)
    counts = jnp.broadcast_to(at_count[:, :, None], (DEV, 2, STEPS)).reshape(NB, 1, LANES)
    tile_h = jnp.arange(HEADS, dtype=jnp.int32)[:, None, None]
    tile_r = jnp.arange(HEADS * TOK, dtype=jnp.int32)[None, :, None]
    tile_k = jnp.arange(JOBS * TOK, dtype=jnp.int32)[None, None, :]
    tile = ((tile_r // TOK == tile_h) & (tile_r % TOK == tile_k % TOK)).astype(BF)
    lane = jnp.arange(BATCH * ROWS, dtype=jnp.int32)
    lane_req = (lane // ROWS) * RD + lane % RD
    lane_step = (lane // RD) % STEPS
    steps = jnp.arange(STEPS, dtype=jnp.int32)
    sel = (full[:, :, None, None] == lane_req) & (steps[None, None, :, None] == lane_step)
    sel = sel.astype(BF).reshape(DEV * 2 * STEPS, BATCH * ROWS)
    part = owner_attention(at_slot.reshape(-1), counts, sel, tile, gathered, kv_store)
    got = lax.all_to_all(part.reshape(DEV, 2 * STEPS, BLK), ("req", "page"), 0, 0, tiled=True)

    own_hit = (t_count > 0).astype(jnp.int32)
    own_rank = jnp.cumsum(own_hit, axis=0) - own_hit
    places = []
    for c in range(2):
        here = (own_hit > 0) & (own_rank == c)
        places.append(jnp.sum(jnp.where(here, request + 1, 0), axis=0) - 1)
    places = jnp.stack(places, axis=1)[:, :, None]
    own = jnp.where(places >= 0, steps[None, None, :] * RD + places, -1).reshape(1, DEV * 2 * STEPS)
    attn = combine(own, got.reshape(DEV * 2 * STEPS, BLK), o, m, l)
    return attn.reshape(STEPS, RD, FEAT), mamba_out.reshape(STEPS, RD, MF)


def solution(mesh):
    in_specs = (
        P(("req", "page"), None, None, None),
        P(("req", "page"), None, None, None),
        P(None, ("req", "page"), None, None),
        P(("req", "page"), None),
        P(("req", "page"), None),
        P(("req", "page")),
        P("page", None, None, None),
        P("req"),
        P(None, ("req", "page"), None),
        P(None, ("req", "page"), None),
        P(None, ("req", "page"), None),
        P(),
    )
    out_specs = (P(None, ("req", "page"), None), P(None, ("req", "page"), None))
    return jax.shard_map(
        on_device, mesh=mesh, in_specs=in_specs, out_specs=out_specs, check_vma=False
    )
```

```python
import functools
import math

import jax
import jax.numpy as jnp
from jax import lax
from jax.experimental import pallas as pl
from jax.experimental.pallas import tpu as pltpu
from jax.sharding import PartitionSpec as P

HEADS = 16
HD = 128
STEPS = 4
RD = 4
ROWS = STEPS * RD
FEAT = HEADS * HD
DEV = 128
TOK = 8
MH = 64
MD = 64
ST = 128
MF = MH * MD
NPG = 8
GRP = 16
PAGES = 64
JOBS = 2 * GRP
KEYS = JOBS * TOK
NEAR = 8
QROWS = 40
NEG = -1e30
SCALE = 1.0 / math.sqrt(HD)
BF = jnp.bfloat16
F32 = jnp.float32
NT = (((1,), (1,)), ((), ()))
NN = (((1,), (0,)), ((), ()))


def dot(a, b, dims=NN):
    return lax.dot_general(a, b, dims, preferred_element_type=F32)


def split2(x):
    hi = x.astype(BF)
    return hi, (x - hi.astype(F32)).astype(BF)


def split3(x):
    hi = x.astype(BF)
    rest = x - hi.astype(F32)
    mid = rest.astype(BF)
    return hi, mid, (rest - mid.astype(F32)).astype(BF)


def local_kernel(q_ref, nk_ref, nv_ref, kv_ref, o_ref, m_ref, l_ref):
    q = q_ref[...]
    parts = [dot(q, kv_ref[r, 0], NT) for r in range(RD)]
    row = lax.broadcasted_iota(jnp.int32, (ROWS, 1), 0)
    keep = row % RD
    new = dot(q, nk_ref[...], NT) * SCALE
    col = lax.broadcasted_iota(jnp.int32, (ROWS, ROWS), 1)
    ok = (col % RD == keep) & (col // RD <= row // RD)
    new = jnp.where(ok, new, NEG)
    mine = jnp.where(keep == 0, parts[0], NEG)
    for r in range(1, RD):
        mine = jnp.where(keep == r, parts[r], mine)
    mine = mine * SCALE
    top = jnp.maximum(jnp.max(mine, axis=1, keepdims=True), jnp.max(new, axis=1, keepdims=True))
    p = jnp.exp(mine - top)
    pn = jnp.where(ok, jnp.exp(new - top), 0.0)
    total = jnp.sum(p, axis=1, keepdims=True) + jnp.sum(pn, axis=1, keepdims=True)
    out = dot(pn.astype(BF), nv_ref[...])
    for r in range(RD):
        out = out + dot(jnp.where(keep == r, p, 0.0).astype(BF), kv_ref[r, 1])
    o_ref[...] = out
    m_ref[...] = jnp.broadcast_to(top, (ROWS, HD))
    l_ref[...] = jnp.broadcast_to(total, (ROWS, HD))


def local_attention(q, nk, nv, local_kv):
    row = pl.BlockSpec((ROWS, HD), lambda h: (0, h))
    return pl.pallas_call(
        local_kernel,
        grid=(HEADS,),
        in_specs=[row, row, row, pl.BlockSpec((RD, 2, 256, HD), lambda h: (0, 0, 0, h))],
        out_specs=[row, row, row],
        out_shape=[jax.ShapeDtypeStruct((ROWS, FEAT), F32)] * 3,
        cost_estimate=pl.CostEstimate(flops=2 * 2 * 16 * 1024 * 2048, bytes_accessed=9_000_000, transcendentals=300_000),
        name="local_attention",
    )(q, nk, nv, local_kv)


def owner_kernel(page_ref, req_ref, q_ref, kv_ref, o_ref, kbuf, vbuf):
    step = pl.program_id(0)
    for d in range(NEAR):
        base = (step * NEAR + d) * JOBS
        for j in range(JOBS):
            page = page_ref[base + j]
            kbuf[d, j] = kv_ref[page, 0]
            vbuf[d, j] = kv_ref[page, 1]
    row = lax.broadcasted_iota(jnp.int32, (1, ROWS, 1), 1)
    ok = row % RD == req_ref[...]
    s = [dot(q_ref[d, :ROWS], kbuf[d].reshape(KEYS, HD), NT)[None] for d in range(NEAR)]
    s = jnp.where(ok, jnp.concatenate(s, axis=0) * SCALE, NEG)
    top = jnp.max(s, axis=2, keepdims=True)
    p = jnp.where(ok, jnp.exp(s - top), 0.0)
    total = jnp.sum(p, axis=2, keepdims=True)
    p = p.astype(BF)
    lane = lax.broadcasted_iota(jnp.int32, (NEAR, ROWS, HD), 2)
    stats = jnp.zeros((NEAR, ROWS, HD), F32)
    for i, part in enumerate(list(split3(top)) + list(split2(total))):
        stats = jnp.where(lane == i, part.astype(F32), stats)
    o_ref[:, :, HD:] = stats.astype(BF)
    for d in range(NEAR):
        o_ref[d, :, :HD] = dot(p[d], vbuf[d].reshape(KEYS, HD)).astype(BF)


def owner_attention(pages, reqs, got, store):
    return pl.pallas_call(
        owner_kernel,
        grid_spec=pltpu.PrefetchScalarGridSpec(
            num_scalar_prefetch=1,
            grid=(DEV // NEAR,),
            in_specs=[
                pl.BlockSpec((NEAR, 1, KEYS), lambda i, s: (i, 0, 0)),
                pl.BlockSpec((NEAR, QROWS, HD), lambda i, s: (i, 0, 0)),
                pl.BlockSpec(store.shape, lambda i, s: (0, 0, 0, 0), pipeline_mode=pl.Buffered(1)),
            ],
            out_specs=pl.BlockSpec((NEAR, ROWS, 2 * HD), lambda i, s: (i, 0, 0)),
            scratch_shapes=[
                pltpu.VMEM((NEAR, JOBS, TOK, HD), BF),
                pltpu.VMEM((NEAR, JOBS, TOK, HD), BF),
            ],
        ),
        out_shape=jax.ShapeDtypeStruct((DEV, ROWS, 2 * HD), BF),
        cost_estimate=pl.CostEstimate(flops=4 * 2048 * 256 * 128, bytes_accessed=8_000_000, transcendentals=600_000),
        compiler_params=pltpu.CompilerParams(vmem_limit_bytes=32 * 1024 * 1024),
        name="owner_attention",
    )(pages, reqs, got, store)


def combine_kernel(got_ref, o_ref, m_ref, l_ref, out_ref):
    stats = got_ref[:, :, HD:].reshape(NPG * ROWS, HD)
    lane = lax.broadcasted_iota(jnp.int32, (HD, HD), 0)
    top = dot(stats, (lane < 3).astype(BF)).reshape(NPG, ROWS, HD)
    total = dot(stats, ((lane >= 3) & (lane < 5)).astype(BF)).reshape(NPG, ROWS, HD)
    got = got_ref[:, :, :HD].astype(F32)
    lm = m_ref[...]
    best = jnp.maximum(jnp.max(top, axis=0), lm)
    w = jnp.exp(top - best[None])
    mine = jnp.exp(lm - best)
    mix = jnp.sum(w * got, axis=0) + mine * o_ref[...]
    out_ref[...] = (mix / (jnp.sum(w * total, axis=0) + mine * l_ref[...])).astype(BF)


def combine(got, o, m, l):
    row = pl.BlockSpec((ROWS, HD), lambda h: (0, h))
    return pl.pallas_call(
        combine_kernel,
        grid=(HEADS,),
        in_specs=[pl.BlockSpec((NPG, ROWS, 2 * HD), lambda h: (h, 0, 0)), row, row, row],
        out_specs=row,
        out_shape=jax.ShapeDtypeStruct((ROWS, FEAT), BF),
        cost_estimate=pl.CostEstimate(flops=4 * 16 * 1024 * 2048, bytes_accessed=2_000_000, transcendentals=300_000),
        name="combine_attention",
    )(got, o, m, l)


def state_kernel(br_ref, c_ref, st_ref, out_ref):
    c = c_ref[...]
    first = dot(c, st_ref[0], NT)
    second = dot(c, st_ref[1], NT)
    which = br_ref[...]
    z = jnp.where(which == 0, first, 0.0) + jnp.where(which == 1, second, 0.0)
    out_ref[...] = z.astype(BF)


def state_products(which, c_all, states):
    wide = 1024
    return pl.pallas_call(
        state_kernel,
        grid=(MF // wide,),
        in_specs=[
            pl.BlockSpec((NPG * ROWS, 1), lambda i: (0, 0)),
            pl.BlockSpec((NPG * ROWS, ST), lambda i: (0, 0)),
            pl.BlockSpec((2, wide, ST), lambda i: (0, i, 0)),
        ],
        out_specs=pl.BlockSpec((NPG * ROWS, wide), lambda i: (0, i)),
        out_shape=jax.ShapeDtypeStruct((NPG * ROWS, MF), BF),
        cost_estimate=pl.CostEstimate(flops=4 * 128 * 128 * 4096, bytes_accessed=3_200_000, transcendentals=0),
        name="state_products",
    )(which, c_all, states)


def scan_kernel(coef_ref, x_ref, z_ref, out_ref):
    wide = out_ref.shape[1]
    head = lax.broadcasted_iota(jnp.int32, (MH, wide), 0)
    chan = lax.broadcasted_iota(jnp.int32, (MH, wide), 1) + pl.program_id(0) * wide
    spread = (head == chan // MD).astype(BF)
    hi, mid, lo = split3(coef_ref[...])
    coef = dot(hi, spread) + dot(mid, spread) + dot(lo, spread)
    y = coef[:ROWS] * z_ref[...].astype(F32)
    x = x_ref[...].astype(F32)
    for t in range(STEPS):
        xt = jnp.concatenate([x[t * RD : (t + 1) * RD]] * STEPS, axis=0)
        y = y + coef[(t + 1) * ROWS : (t + 2) * ROWS] * xt
    out_ref[...] = y.astype(BF)


def scan_outputs(coef, x, z):
    wide = 1024
    spec = pl.BlockSpec((ROWS, wide), lambda i: (0, i))
    return pl.pallas_call(
        scan_kernel,
        grid=(MF // wide,),
        in_specs=[pl.BlockSpec(coef.shape, lambda i: (0, 0))] + [spec] * 2,
        out_specs=spec,
        out_shape=jax.ShapeDtypeStruct((ROWS, MF), BF),
        cost_estimate=pl.CostEstimate(flops=6 * 80 * 64 * 4096, bytes_accessed=1_500_000, transcendentals=0),
        name="scan_outputs",
    )(coef, x, z)


def coefficients(mamba_bc, mamba_dt, decay_rate):
    delta = jax.nn.softplus(mamba_dt.astype(F32))
    rate = -decay_rate[None, :] * delta
    decay = jnp.exp(rate)
    b, c = mamba_bc[:, :, :ST], mamba_bc[:, :, ST:]
    bc = jnp.einsum("trn,srn->tsr", b, c, preferred_element_type=F32)
    rows = []
    run = decay[0]
    for s in range(STEPS):
        rows.append(run)
        if s + 1 < STEPS:
            run = run * decay[s + 1]
    zero = jnp.zeros_like(run)
    for t in range(STEPS):
        carry = delta[t]
        for s in range(STEPS):
            if s < t:
                rows.append(zero)
                continue
            if s > t:
                carry = carry * decay[s]
            rows.append(carry * bc[t, s][:, None])
    return jnp.stack(rows).reshape((1 + STEPS) * ROWS, MH)


def on_device(
    kv_store,
    local_kv,
    new_qkv,
    page_owner,
    page_slot,
    prefix_len,
    prefix_states,
    branch_id,
    mamba_x,
    mamba_bc,
    mamba_dt,
    decay_rate,
):
    my_req, my_page = lax.axis_index("req"), lax.axis_index("page")
    q = new_qkv[:, :, 0].reshape(ROWS, FEAT)
    nk = new_qkv[:, :, 1].reshape(ROWS, FEAT)
    nv = new_qkv[:, :, 2].reshape(ROWS, FEAT)

    count = jnp.clip(prefix_len[:, None] - TOK * jnp.arange(page_owner.shape[1], dtype=jnp.int32)[None, :], 0, TOK)
    named = page_owner[:, :, None] == jnp.arange(DEV, dtype=jnp.int32)[None, None, :]
    t_slot = jnp.sum(jnp.where(named, page_slot[:, :, None], 0), axis=1)
    t_count = jnp.sum(jnp.where(named, count[:, :, None], 0), axis=1)
    tables = jnp.stack([t_slot, t_count]).reshape(2, RD, GRP, NPG).transpose(3, 0, 1, 2).reshape(NPG, 1, HD).astype(BF)
    tables = jnp.broadcast_to(jnp.pad(tables, ((0, 0), (0, TOK - 1), (0, 0)))[None], (GRP, NPG, TOK, HD))
    heads = jnp.broadcast_to(q.reshape(ROWS, HEADS, HD).transpose(1, 0, 2)[:, None], (GRP, NPG, ROWS, HD))
    c_own = jnp.broadcast_to(mamba_bc[:, :, ST:].reshape(1, 1, ROWS, ST), (GRP, NPG, ROWS, ST))
    sent = jnp.concatenate([heads, c_own, tables], axis=2).reshape(DEV, QROWS, HD)
    got_q = lax.all_to_all(sent, ("req", "page"), 0, 0, tiled=True)

    store = kv_store.reshape(PAGES, 2, TOK, HEADS, HD).transpose(3, 0, 1, 2, 4)
    store = lax.all_to_all(store, "req", 0, 0, tiled=True).reshape(GRP * PAGES, 2, TOK, HD)

    c_all = lax.dynamic_slice_in_dim(got_q, my_req * NPG, NPG)[:, ROWS : 2 * ROWS].reshape(NPG * ROWS, ST)
    branch = branch_id.reshape(NPG, 1, RD) - 2 * my_page
    branch = jnp.broadcast_to(branch, (NPG, STEPS, RD)).reshape(NPG * ROWS, 1)
    z = state_products(branch, c_all, prefix_states.reshape(2, MF, ST))
    z = lax.psum_scatter(z.reshape(NPG, ROWS, MF), "page", scatter_dimension=0, tiled=True)
    coef = coefficients(mamba_bc, mamba_dt, decay_rate)
    mamba_out = scan_outputs(coef, mamba_x.reshape(ROWS, MF), z.reshape(ROWS, MF))

    o, m, l = local_attention(q, nk, nv, local_kv)

    table = got_q[:, 2 * ROWS].astype(jnp.int32).reshape(DEV, 2, RD, GRP)
    c_slot, c_count = table[:, 0], table[:, 1]
    hit = (c_count > 0).astype(jnp.int32)
    rank = jnp.cumsum(hit, axis=1) - hit
    request = jnp.arange(RD, dtype=jnp.int32)[None, :, None]
    at_slot, at_req, at_count = [], [], []
    for c in range(2):
        here = (hit > 0) & (rank == c)
        at_slot.append(jnp.sum(jnp.where(here, c_slot, 0), axis=1))
        at_count.append(jnp.sum(jnp.where(here, c_count, 0), axis=1))
        at_req.append(jnp.sum(jnp.where(here, request, 0), axis=1))
    owner = jnp.arange(GRP, dtype=jnp.int32)[None, None, :]
    pages = (jnp.stack(at_slot, axis=1) + PAGES * owner).reshape(DEV * JOBS)
    tok = jnp.arange(TOK, dtype=jnp.int32)
    reqs = jnp.where(tok < jnp.stack(at_count, axis=1)[..., None], jnp.stack(at_req, axis=1)[..., None], -1)
    store, o, m, l = lax.optimization_barrier((store, o, m, l))
    part = owner_attention(pages, reqs.reshape(DEV, 1, KEYS), got_q, store)
    got = lax.all_to_all(part, ("req", "page"), 0, 0, tiled=True)
    attn = combine(got, o, m, l)
    return attn.reshape(STEPS, RD, FEAT), mamba_out.reshape(STEPS, RD, MF)


def solution(mesh):
    in_specs = (
        P(("req", "page"), None, None, None),
        P(("req", "page"), None, None, None),
        P(None, ("req", "page"), None, None),
        P(("req", "page"), None),
        P(("req", "page"), None),
        P(("req", "page")),
        P("page", None, None, None),
        P("req"),
        P(None, ("req", "page"), None),
        P(None, ("req", "page"), None),
        P(None, ("req", "page"), None),
        P(),
    )
    out_specs = (P(None, ("req", "page"), None), P(None, ("req", "page"), None))
    return jax.shard_map(
        on_device, mesh=mesh, in_specs=in_specs, out_specs=out_specs, check_vma=False
    )
```

```python
import functools
import math

import jax
import jax.numpy as jnp
from jax import lax
from jax.experimental import pallas as pl
from jax.experimental.pallas import tpu as pltpu
from jax.sharding import PartitionSpec as P

HEADS = 16
HD = 128
STEPS = 4
RD = 4
ROWS = STEPS * RD
FEAT = HEADS * HD
DEV = 128
TOK = 8
MH = 64
MD = 64
ST = 128
MF = MH * MD
NPG = 8
PAGES = 64
JOBS = 32
KEYS = JOBS * TOK
NEAR = 8
TILES = 19
META = 18
HPC = 4
NEG = -1e30
SCALE = 1.0 / math.sqrt(HD)
BF = jnp.bfloat16
F32 = jnp.float32
NT = (((1,), (1,)), ((), ()))
NN = (((1,), (0,)), ((), ()))


def dot(a, b, dims=NN):
    return lax.dot_general(a, b, dims, preferred_element_type=F32)


def split2(x):
    hi = x.astype(BF)
    return hi, (x - hi.astype(F32)).astype(BF)


def split3(x):
    hi = x.astype(BF)
    rest = x - hi.astype(F32)
    mid = rest.astype(BF)
    return hi, mid, (rest - mid.astype(F32)).astype(BF)


def local_kernel(q_ref, nk_ref, nv_ref, kv_ref, o_ref, m_ref, l_ref):
    q = q_ref[...]
    parts = [dot(q, kv_ref[r, 0], NT) for r in range(RD)]
    row = lax.broadcasted_iota(jnp.int32, (ROWS, 1), 0)
    keep = row % RD
    new = dot(q, nk_ref[...], NT) * SCALE
    col = lax.broadcasted_iota(jnp.int32, (ROWS, ROWS), 1)
    ok = (col % RD == keep) & (col // RD <= row // RD)
    new = jnp.where(ok, new, NEG)
    mine = jnp.where(keep == 0, parts[0], NEG)
    for r in range(1, RD):
        mine = jnp.where(keep == r, parts[r], mine)
    mine = mine * SCALE
    top = jnp.maximum(jnp.max(mine, axis=1, keepdims=True), jnp.max(new, axis=1, keepdims=True))
    p = jnp.exp(mine - top)
    pn = jnp.where(ok, jnp.exp(new - top), 0.0)
    total = jnp.sum(p, axis=1, keepdims=True) + jnp.sum(pn, axis=1, keepdims=True)
    out = dot(pn.astype(BF), nv_ref[...])
    for r in range(RD):
        out = out + dot(jnp.where(keep == r, p, 0.0).astype(BF), kv_ref[r, 1])
    o_ref[...] = out
    m_ref[...] = jnp.broadcast_to(top, (ROWS, HD))
    l_ref[...] = jnp.broadcast_to(total, (ROWS, HD))


def local_attention(q, nk, nv, local_kv):
    row = pl.BlockSpec((ROWS, HD), lambda h: (0, h))
    return pl.pallas_call(
        local_kernel,
        grid=(HEADS,),
        in_specs=[row, row, row, pl.BlockSpec((RD, 2, 256, HD), lambda h: (0, 0, 0, h))],
        out_specs=[row, row, row],
        out_shape=[jax.ShapeDtypeStruct((ROWS, FEAT), F32)] * 3,
        cost_estimate=pl.CostEstimate(flops=2 * 2 * 16 * 1024 * 2048, bytes_accessed=9_000_000, transcendentals=300_000),
        name="local_attention",
    )(q, nk, nv, local_kv)


def pack_kernel(len_ref, own_ref, slot_ref, kv_ref, q_ref, out_ref, lists, qbuf):
    g = pl.program_id(0)

    @pl.when(g == 0)
    def _():
        path = own_ref.shape[1]
        lane = lax.broadcasted_iota(jnp.int32, (8, HD), 1)
        row = lax.broadcasted_iota(jnp.int32, (8, HD), 0)
        owner = jnp.concatenate([own_ref[r : r + 1] for r in range(RD)], axis=1)
        slot = jnp.concatenate([slot_ref[r : r + 1] for r in range(RD)], axis=1)
        req = lane // path
        size = jnp.where(req == 0, len_ref[0], len_ref[1])
        size = jnp.where(req == 2, len_ref[2], jnp.where(req == 3, len_ref[3], size))
        count = jnp.clip(size - TOK * (lane % path), 0, TOK)
        vals = jnp.where(row == 0, owner, jnp.where(row == 1, slot % 8, 0))
        vals = jnp.where(row == 2, req + 1, jnp.where(row == 3, count, vals))
        vals = vals.astype(F32).astype(BF)
        inside = (slot // 8 == row) & (count > 0)
        up = lax.broadcasted_iota(jnp.int32, (HD, HD), 0) < lax.broadcasted_iota(jnp.int32, (HD, HD), 1)
        rank = dot(inside.astype(F32).astype(BF), up.astype(F32).astype(BF))
        rank = jnp.transpose(jnp.where(inside, rank, -1.0))
        place = lax.broadcasted_iota(jnp.int32, (HD, HD), 1).astype(F32)
        for i in range(NPG):
            mine = rank[:, i : i + 1]
            out = dot(vals, (mine == place).astype(F32).astype(BF))
            number = jnp.sum((mine >= 0).astype(F32), axis=0, keepdims=True)
            lists[i] = jnp.where(row == 4, number, out).astype(BF)
        for t in range(STEPS):
            qbuf[t * RD : (t + 1) * RD] = q_ref[t, 0].astype(F32)

    mine = lists[g]
    for m in range(HEADS):
        at = slice(m * HD, (m + 1) * HD)
        out_ref[m, 0, :16] = kv_ref[:, :, :, at].reshape(16, TOK, HD)
        out_ref[m, 0, 16:18] = qbuf[:, at].astype(BF).reshape(2, TOK, HD)
        out_ref[m, 0, 18] = mine


def pack(lens, owner, slot, kv_store, qkv):
    whole = lambda x: pl.BlockSpec(x.shape, lambda g, n: (0,) * len(x.shape))
    return pl.pallas_call(
        pack_kernel,
        grid_spec=pltpu.PrefetchScalarGridSpec(
            num_scalar_prefetch=1,
            grid=(NPG,),
            in_specs=[
                whole(owner),
                whole(slot),
                pl.BlockSpec((PAGES // NPG, 2, TOK, FEAT), lambda g, n: (g, 0, 0, 0)),
                whole(qkv),
            ],
            out_specs=pl.BlockSpec((HEADS, 1, TILES, TOK, HD), lambda g, n: (0, g, 0, 0, 0)),
            scratch_shapes=[pltpu.VMEM((NPG, 8, HD), BF), pltpu.VMEM((ROWS, FEAT), F32)],
        ),
        out_shape=jax.ShapeDtypeStruct((HEADS, NPG, TILES, TOK, HD), BF),
        cost_estimate=pl.CostEstimate(flops=1_000_000, bytes_accessed=10_000_000, transcendentals=0),
        name="pack",
    )(lens, owner, slot, kv_store, qkv)


def owner_kernel(got_ref, o_ref, kbuf, vbuf, acc, tops, sums, index, tile_ref, sem):
    step = pl.program_id(0)

    @pl.when(step == 0)
    def _():
        lists = got_ref[pl.ds(META, DEV, stride=TILES)].astype(F32)
        index[:DEV] = (lists[:, 0] * TILES + 2 * lists[:, 1]).astype(jnp.int32)
        index[DEV:] = jnp.transpose(lists[:, 4])[:TOK].astype(jnp.int32)
        copy = pltpu.make_async_copy(index, tile_ref, sem)
        copy.start()
        copy.wait()

    base = step * NEAR

    def fetch(d, at):
        d_all = base + d
        for j in range(JOBS):
            tile = tile_ref[d_all, at + j]
            kbuf[d, j] = got_ref[tile]
            vbuf[d, j] = got_ref[tile + 1]

    def spread(meta, first):
        key = lax.broadcasted_iota(jnp.int32, (HD, KEYS), 1)
        pos = lax.broadcasted_iota(jnp.int32, (HD, KEYS), 0)
        return dot(meta, (pos == first + key // TOK).astype(F32).astype(BF))

    def scores(d, q):
        return dot(q, kbuf[d].reshape(KEYS, HD), NT)

    def mix(d, p):
        return dot(p, vbuf[d].reshape(KEYS, HD))

    def write(dst, top, total, out):
        lane = lax.broadcasted_iota(jnp.int32, top.shape[:-1] + (HD,), top.ndim - 1)
        stats = jnp.zeros(lane.shape, F32)
        for i, part in enumerate(list(split3(top)) + list(split2(total))):
            stats = jnp.where(lane == i, part.astype(F32), stats)
        o_ref[dst, :, HD:] = stats.astype(BF)
        o_ref[dst, :, :HD] = out.astype(BF)

    for d in range(NEAR):
        fetch(d, 0)
    tok = (lax.broadcasted_iota(jnp.int32, (1, KEYS), 1) % TOK).astype(F32)
    want = (lax.broadcasted_iota(jnp.int32, (ROWS, 1), 0) % RD + 1).astype(F32)
    queries = [got_ref[pl.ds((base + d) * TILES + 16, 2)].reshape(ROWS, HD) for d in range(NEAR)]
    meta = jnp.concatenate([got_ref[(base + d) * TILES + META] for d in range(NEAR)], axis=0)
    wide = spread(meta, 0).reshape(NEAR, 8, KEYS)
    ok = (wide[:, 2:3] == want[None]) & (tok[None] < wide[:, 3:4])
    s = jnp.concatenate([scores(d, queries[d])[None] for d in range(NEAR)], axis=0)
    s = jnp.where(ok, s * SCALE, NEG)
    top = jnp.max(s, axis=2, keepdims=True)
    p = jnp.where(ok, jnp.exp(s - top), 0.0)
    total = jnp.sum(p, axis=2, keepdims=True)
    p = p.astype(BF)
    out = jnp.concatenate([mix(d, p[d])[None] for d in range(NEAR)], axis=0)
    write(slice(None), top, total, out)
    most = tile_ref[DEV, base]
    for d in range(1, NEAR):
        most = jnp.maximum(most, tile_ref[DEV, base + d])

    @pl.when(most > JOBS)
    def _():
        acc[...] = out
        tops[...] = jnp.broadcast_to(top, tops.shape)
        sums[...] = jnp.broadcast_to(total, sums.shape)
        for d in range(NEAR):
            num = tile_ref[DEV, base + d]

            @pl.loop(1, (num + JOBS - 1) // JOBS)
            def _(c):
                fetch(d, c * JOBS)
                wide = spread(got_ref[(base + d) * TILES + META], c * JOBS)
                ok = (wide[2:3] == want) & (tok < wide[3:4])
                s = jnp.where(ok, scores(d, got_ref[pl.ds((base + d) * TILES + 16, 2)].reshape(ROWS, HD)) * SCALE, NEG)
                best = jnp.maximum(tops[d], jnp.max(s, axis=1, keepdims=True))
                p = jnp.where(ok, jnp.exp(s - best[:, :1]), 0.0)
                old = jnp.exp(tops[d] - best)
                acc[d] = old * acc[d] + mix(d, p.astype(BF))
                sums[d] = old * sums[d] + jnp.sum(p, axis=1, keepdims=True)
                tops[d] = best

            @pl.when(num > JOBS)
            def _():
                write(d, tops[d], sums[d], acc[d])


def owner_attention(got):
    return pl.pallas_call(
        owner_kernel,
        grid=(DEV // NEAR,),
        in_specs=[pl.BlockSpec(got.shape, lambda i: (0, 0, 0), pipeline_mode=pl.Buffered(1))],
        out_specs=pl.BlockSpec((NEAR, ROWS, 2 * HD), lambda i: (i, 0, 0)),
        scratch_shapes=[
            pltpu.VMEM((NEAR, JOBS, TOK, HD), BF),
            pltpu.VMEM((NEAR, JOBS, TOK, HD), BF),
            pltpu.VMEM((NEAR, ROWS, HD), F32),
            pltpu.VMEM((NEAR, ROWS, HD), F32),
            pltpu.VMEM((NEAR, ROWS, HD), F32),
            pltpu.VMEM((DEV + TOK, HD), jnp.int32),
            pltpu.SMEM((DEV + TOK, HD), jnp.int32),
            pltpu.SemaphoreType.DMA,
        ],
        out_shape=jax.ShapeDtypeStruct((DEV, ROWS, 2 * HD), BF),
        cost_estimate=pl.CostEstimate(flops=4 * 2048 * 256 * 128, bytes_accessed=8_000_000, transcendentals=600_000),
        compiler_params=pltpu.CompilerParams(vmem_limit_bytes=32 * 1024 * 1024),
        name="owner_attention",
    )(got)


def combine_kernel(got_ref, o_ref, m_ref, l_ref, out_ref):
    lane = lax.broadcasted_iota(jnp.int32, (HD, HD), 0)
    top_of = (lane < 3).astype(F32).astype(BF)
    sum_of = ((lane >= 3) & (lane < 5)).astype(F32).astype(BF)
    stats = got_ref[:, :, HD:].reshape(HPC * NPG * ROWS, HD)
    tops = dot(stats, top_of).reshape(HPC, NPG, ROWS, HD)
    sums = dot(stats, sum_of).reshape(HPC, NPG, ROWS, HD)
    for h in range(HPC):
        at = slice(h * HD, (h + 1) * HD)
        got = got_ref[h * NPG : (h + 1) * NPG, :, :HD].astype(F32)
        lm = m_ref[:, at]
        best = jnp.maximum(jnp.max(tops[h], axis=0), lm)
        w = jnp.exp(tops[h] - best[None])
        mine = jnp.exp(lm - best)
        mixed = jnp.sum(w * got, axis=0) + mine * o_ref[:, at]
        mixed = (mixed / (jnp.sum(w * sums[h], axis=0) + mine * l_ref[:, at])).astype(BF)
        for t in range(STEPS):
            out_ref[t, :, at] = mixed[t * RD : (t + 1) * RD]


def combine(got, o, m, l):
    row = pl.BlockSpec((ROWS, HPC * HD), lambda h: (0, h))
    return pl.pallas_call(
        combine_kernel,
        grid=(HEADS // HPC,),
        in_specs=[pl.BlockSpec((HPC * NPG, ROWS, 2 * HD), lambda h: (h, 0, 0)), row, row, row],
        out_specs=pl.BlockSpec((STEPS, RD, HPC * HD), lambda h: (0, 0, h)),
        out_shape=jax.ShapeDtypeStruct((STEPS, RD, FEAT), BF),
        cost_estimate=pl.CostEstimate(flops=4 * 16 * 1024 * 2048, bytes_accessed=2_000_000, transcendentals=300_000),
        name="combine_attention",
    )(got, o, m, l)


def state_kernel(br_ref, c_ref, st_ref, out_ref):
    c = c_ref[...]
    first = dot(c, st_ref[0], NT)
    second = dot(c, st_ref[1], NT)
    which = br_ref[...]
    z = jnp.where(which == 0, first, 0.0) + jnp.where(which == 1, second, 0.0)
    out_ref[...] = z.astype(BF)


def state_products(which, c_all, states):
    wide = 1024
    return pl.pallas_call(
        state_kernel,
        grid=(MF // wide,),
        in_specs=[
            pl.BlockSpec((NPG * ROWS, 1), lambda i: (0, 0)),
            pl.BlockSpec((NPG * ROWS, ST), lambda i: (0, 0)),
            pl.BlockSpec((2, wide, ST), lambda i: (0, i, 0)),
        ],
        out_specs=pl.BlockSpec((NPG * ROWS, wide), lambda i: (0, i)),
        out_shape=jax.ShapeDtypeStruct((NPG * ROWS, MF), BF),
        cost_estimate=pl.CostEstimate(flops=4 * 128 * 128 * 4096, bytes_accessed=3_200_000, transcendentals=0),
        name="state_products",
    )(which, c_all, states)


def scan_kernel(coef_ref, x_ref, z_ref, out_ref):
    wide = out_ref.shape[2]
    head = lax.broadcasted_iota(jnp.int32, (MH, wide), 0)
    chan = lax.broadcasted_iota(jnp.int32, (MH, wide), 1) + pl.program_id(0) * wide
    spread = (head == chan // MD).astype(BF)
    hi, mid, lo = split3(coef_ref[...])
    coef = dot(hi, spread) + dot(mid, spread) + dot(lo, spread)
    y = coef[:ROWS] * z_ref[...].astype(F32)
    x = x_ref[...].astype(F32)
    for t in range(STEPS):
        xt = jnp.concatenate([x[t * RD : (t + 1) * RD]] * STEPS, axis=0)
        y = y + coef[(t + 1) * ROWS : (t + 2) * ROWS] * xt
    y = y.astype(BF)
    for t in range(STEPS):
        out_ref[t] = y[t * RD : (t + 1) * RD]


def scan_outputs(coef, x, z):
    wide = 1024
    spec = pl.BlockSpec((ROWS, wide), lambda i: (0, i))
    return pl.pallas_call(
        scan_kernel,
        grid=(MF // wide,),
        in_specs=[pl.BlockSpec(coef.shape, lambda i: (0, 0))] + [spec] * 2,
        out_specs=pl.BlockSpec((STEPS, RD, wide), lambda i: (0, 0, i)),
        out_shape=jax.ShapeDtypeStruct((STEPS, RD, MF), BF),
        cost_estimate=pl.CostEstimate(flops=6 * 80 * 64 * 4096, bytes_accessed=1_500_000, transcendentals=0),
        name="scan_outputs",
    )(coef, x, z)


def coefficients(mamba_bc, mamba_dt, decay_rate):
    delta = jax.nn.softplus(mamba_dt.astype(F32))
    rate = -decay_rate[None, :] * delta
    decay = jnp.exp(rate)
    b, c = mamba_bc[:, :, :ST], mamba_bc[:, :, ST:]
    bc = jnp.einsum("trn,srn->tsr", b, c, preferred_element_type=F32)
    rows = []
    run = decay[0]
    for s in range(STEPS):
        rows.append(run)
        if s + 1 < STEPS:
            run = run * decay[s + 1]
    zero = jnp.zeros_like(run)
    for t in range(STEPS):
        carry = delta[t]
        for s in range(STEPS):
            if s < t:
                rows.append(zero)
                continue
            if s > t:
                carry = carry * decay[s]
            rows.append(carry * bc[t, s][:, None])
    return jnp.stack(rows).reshape((1 + STEPS) * ROWS, MH)


def on_device(
    kv_store,
    local_kv,
    new_qkv,
    page_owner,
    page_slot,
    prefix_len,
    prefix_states,
    branch_id,
    mamba_x,
    mamba_bc,
    mamba_dt,
    decay_rate,
):
    my_page = lax.axis_index("page")
    q = new_qkv[:, :, 0].reshape(ROWS, FEAT)
    nk = new_qkv[:, :, 1].reshape(ROWS, FEAT)
    nv = new_qkv[:, :, 2].reshape(ROWS, FEAT)

    x_own = mamba_x.reshape(ROWS, MF)
    c_own = jnp.concatenate([mamba_bc[:, :, ST:].reshape(ROWS, ST), x_own], axis=1)
    c_all = lax.all_gather(c_own, "page", axis=0, tiled=True)
    branch = branch_id.reshape(NPG, 1, RD) - 2 * my_page
    branch = jnp.broadcast_to(branch, (NPG, STEPS, RD)).reshape(NPG * ROWS, 1)
    z = state_products(branch, c_all, prefix_states.reshape(2, MF, ST))
    z = lax.psum_scatter(z.reshape(NPG, ROWS, MF), "page", scatter_dimension=0, tiled=True)

    sent = pack(prefix_len, page_owner, page_slot, kv_store, new_qkv.transpose(0, 2, 1, 3))
    got_q = lax.all_to_all(sent.reshape(DEV, TILES, TOK, HD), ("req", "page"), 0, 0, tiled=True)

    coef = coefficients(mamba_bc, mamba_dt, decay_rate)
    mamba_out = scan_outputs(coef, x_own, z.reshape(ROWS, MF))

    o, m, l = local_attention(q, nk, nv, local_kv)

    got_q, o, m, l = lax.optimization_barrier((got_q, o, m, l))
    part = owner_attention(got_q.reshape(DEV * TILES, TOK, HD))
    got = lax.all_to_all(part, ("req", "page"), 0, 0, tiled=True)
    attn = combine(got, o, m, l)
    return attn, mamba_out


def solution(mesh):
    in_specs = (
        P(("req", "page"), None, None, None),
        P(("req", "page"), None, None, None),
        P(None, ("req", "page"), None, None),
        P(("req", "page"), None),
        P(("req", "page"), None),
        P(("req", "page")),
        P("page", None, None, None),
        P("req"),
        P(None, ("req", "page"), None),
        P(None, ("req", "page"), None),
        P(None, ("req", "page"), None),
        P(),
    )
    out_specs = (P(None, ("req", "page"), None), P(None, ("req", "page"), None))
    return jax.shard_map(
        on_device, mesh=mesh, in_specs=in_specs, out_specs=out_specs, check_vma=False
    )
```

```python
import functools
import math

import jax
import jax.numpy as jnp
from jax import lax
from jax.experimental import pallas as pl
from jax.experimental.pallas import tpu as pltpu
from jax.sharding import PartitionSpec as P

HEADS = 16
HD = 128
STEPS = 4
RD = 4
ROWS = STEPS * RD
FEAT = HEADS * HD
DEV = 128
TOK = 8
MH = 64
MD = 64
ST = 128
MF = MH * MD
NPG = 8
PAGES = 64
JOBS = 32
KEYS = JOBS * TOK
NEAR = 16
TILES = 19
META = 18
NEG = -1e30
VMEM_LIMIT = 20 * 1024 * 1024
SCALE = 1.0 / math.sqrt(HD)
BF = jnp.bfloat16
F32 = jnp.float32
NT = (((1,), (1,)), ((), ()))
NN = (((1,), (0,)), ((), ()))


def dot(a, b, dims=NN):
    return lax.dot_general(a, b, dims, preferred_element_type=F32)


def split2(x):
    hi = x.astype(BF)
    return hi, (x - hi.astype(F32)).astype(BF)


def split3(x):
    hi = x.astype(BF)
    rest = x - hi.astype(F32)
    mid = rest.astype(BF)
    return hi, mid, (rest - mid.astype(F32)).astype(BF)


def local_kernel(q_ref, nk_ref, nv_ref, kv_ref, o_ref, m_ref, l_ref):
    q = q_ref[...]
    parts = [dot(q, kv_ref[r, 0], NT) for r in range(RD)]
    row = lax.broadcasted_iota(jnp.int32, (ROWS, 1), 0)
    keep = row % RD
    new = dot(q, nk_ref[...], NT) * SCALE
    col = lax.broadcasted_iota(jnp.int32, (ROWS, ROWS), 1)
    ok = (col % RD == keep) & (col // RD <= row // RD)
    new = jnp.where(ok, new, NEG)
    mine = jnp.where(keep == 0, parts[0], NEG)
    for r in range(1, RD):
        mine = jnp.where(keep == r, parts[r], mine)
    mine = mine * SCALE
    top = jnp.maximum(jnp.max(mine, axis=1, keepdims=True), jnp.max(new, axis=1, keepdims=True))
    p = jnp.exp(mine - top)
    pn = jnp.where(ok, jnp.exp(new - top), 0.0)
    total = jnp.sum(p, axis=1, keepdims=True) + jnp.sum(pn, axis=1, keepdims=True)
    out = dot(pn.astype(BF), nv_ref[...])
    for r in range(RD):
        out = out + dot(jnp.where(keep == r, p, 0.0).astype(BF), kv_ref[r, 1])
    o_ref[...] = out
    m_ref[...] = jnp.broadcast_to(top, (ROWS, HD))
    l_ref[...] = jnp.broadcast_to(total, (ROWS, HD))


def local_attention(q, nk, nv, local_kv):
    row = pl.BlockSpec((ROWS, HD), lambda h: (0, h))
    return pl.pallas_call(
        local_kernel,
        grid=(HEADS,),
        in_specs=[row, row, row, pl.BlockSpec((RD, 2, 256, HD), lambda h: (0, 0, 0, h))],
        out_specs=[row, row, row],
        out_shape=[jax.ShapeDtypeStruct((ROWS, FEAT), F32)] * 3,
        cost_estimate=pl.CostEstimate(flops=2 * 2 * 16 * 1024 * 2048, bytes_accessed=9_000_000, transcendentals=300_000),
        compiler_params=pltpu.CompilerParams(vmem_limit_bytes=VMEM_LIMIT),
        name="local_attention",
    )(q, nk, nv, local_kv)


def pack_kernel(len_ref, own_ref, slot_ref, kv_ref, q_ref, out_ref, buf, lists, qbuf, sem):
    copies = []
    for m in range(HEADS):
        src = kv_ref.at[:, :, :, pl.ds(m * HD, HD)]
        copies.append(pltpu.make_async_copy(src, buf.at[m, :, pl.ds(0, 16)], sem.at[0, m]))
        copies[-1].start()
    path = own_ref.shape[1]
    lane = lax.broadcasted_iota(jnp.int32, (8, HD), 1)
    row = lax.broadcasted_iota(jnp.int32, (8, HD), 0)
    owner = jnp.concatenate([own_ref[r : r + 1] for r in range(RD)], axis=1)
    slot = jnp.concatenate([slot_ref[r : r + 1] for r in range(RD)], axis=1)
    req = lane // path
    size = jnp.where(req == 0, len_ref[0], len_ref[1])
    size = jnp.where(req == 2, len_ref[2], jnp.where(req == 3, len_ref[3], size))
    count = jnp.clip(size - TOK * (lane % path), 0, TOK)
    vals = jnp.where(row == 0, owner, jnp.where(row == 1, slot % 8, 0))
    vals = jnp.where(row == 2, req + 1, jnp.where(row == 3, count, vals))
    vals = vals.astype(F32).astype(BF)
    inside = (slot // 8 == row) & (count > 0)
    up = lax.broadcasted_iota(jnp.int32, (HD, HD), 0) < lax.broadcasted_iota(jnp.int32, (HD, HD), 1)
    rank = dot(inside.astype(F32).astype(BF), up.astype(F32).astype(BF))
    rank = jnp.transpose(jnp.where(inside, rank, -1.0))
    place = lax.broadcasted_iota(jnp.int32, (HD, HD), 1).astype(F32)
    for i in range(NPG):
        mine = rank[:, i : i + 1]
        out = dot(vals, (mine == place).astype(F32).astype(BF))
        number = jnp.sum((mine >= 0).astype(F32), axis=0, keepdims=True)
        lists[i] = jnp.where(row == 4, number, out).astype(BF)
    for t in range(STEPS):
        qbuf[t * RD : (t + 1) * RD] = q_ref[t, 0].astype(F32)

    for m in range(HEADS):
        at = slice(m * HD, (m + 1) * HD)
        q = qbuf[:, at].astype(BF).reshape(1, 2, TOK, HD)
        buf[m, :, 16:18] = jnp.broadcast_to(q, (NPG, 2, TOK, HD))
        buf[m, :, META] = lists[...]
    back = []
    for m in range(HEADS):
        copies[m].wait()
        back.append(pltpu.make_async_copy(buf.at[m], out_ref.at[m], sem.at[1, m]))
        back[-1].start()
    for copy in back:
        copy.wait()


def pack(lens, owner, slot, kv_store, qkv):
    vmem = pl.BlockSpec(memory_space=pltpu.VMEM)
    return pl.pallas_call(
        pack_kernel,
        in_specs=[pl.BlockSpec(memory_space=pltpu.SMEM), vmem, vmem, pl.BlockSpec(memory_space=pl.ANY), vmem],
        out_specs=pl.BlockSpec(memory_space=pl.ANY),
        scratch_shapes=[
            pltpu.VMEM((HEADS, NPG, TILES, TOK, HD), BF),
            pltpu.VMEM((NPG, TOK, HD), BF),
            pltpu.VMEM((ROWS, FEAT), F32),
            pltpu.SemaphoreType.DMA((2, HEADS)),
        ],
        out_shape=jax.ShapeDtypeStruct((HEADS, NPG, TILES, TOK, HD), BF),
        cost_estimate=pl.CostEstimate(flops=1_000_000, bytes_accessed=10_000_000, transcendentals=0),
        name="pack",
    )(lens, owner, slot, kv_store.reshape(NPG, 16, TOK, FEAT), qkv)


def owner_kernel(got_ref, o_ref, kbuf, vbuf, acc, tops, sums, index, tile_ref, sem):
    step = pl.program_id(0)

    @pl.when(step == 0)
    def _():
        lists = got_ref[pl.ds(META, DEV, stride=TILES)].astype(F32)
        index[:DEV] = (lists[:, 0] * TILES + 2 * lists[:, 1]).astype(jnp.int32)
        index[DEV:] = jnp.transpose(lists[:, 4])[:TOK].astype(jnp.int32)
        copy = pltpu.make_async_copy(index, tile_ref, sem)
        copy.start()
        copy.wait()

    base = step * NEAR

    def fetch(d, at):
        d_all = base + d
        for j in range(JOBS):
            tile = tile_ref[d_all, at + j]
            kbuf[d, j] = got_ref[tile]
            vbuf[d, j] = got_ref[tile + 1]

    def spread(meta, first):
        key = lax.broadcasted_iota(jnp.int32, (HD, KEYS), 1)
        pos = lax.broadcasted_iota(jnp.int32, (HD, KEYS), 0)
        return dot(meta, (pos == first + key // TOK).astype(F32).astype(BF))

    def scores(d, q):
        return dot(q, kbuf[d].reshape(KEYS, HD), NT)

    def mix(d, p):
        return dot(p, vbuf[d].reshape(KEYS, HD))

    def write(dst, top, total, out):
        lane = lax.broadcasted_iota(jnp.int32, top.shape[:-1] + (HD,), top.ndim - 1)
        stats = jnp.zeros(lane.shape, F32)
        for i, part in enumerate(list(split3(top)) + list(split2(total))):
            stats = jnp.where(lane == i, part.astype(F32), stats)
        o_ref[dst, :, HD:] = stats.astype(BF)
        o_ref[dst, :, :HD] = out.astype(BF)

    for d in range(NEAR):
        fetch(d, 0)
    tok = (lax.broadcasted_iota(jnp.int32, (1, KEYS), 1) % TOK).astype(F32)
    want = (lax.broadcasted_iota(jnp.int32, (ROWS, 1), 0) % RD + 1).astype(F32)
    queries = [got_ref[pl.ds((base + d) * TILES + 16, 2)].reshape(ROWS, HD) for d in range(NEAR)]
    meta = jnp.concatenate([got_ref[(base + d) * TILES + META] for d in range(NEAR)], axis=0)
    wide = spread(meta, 0).reshape(NEAR, 8, KEYS)
    ok = (wide[:, 2:3] == want[None]) & (tok[None] < wide[:, 3:4])
    s = jnp.concatenate([scores(d, queries[d])[None] for d in range(NEAR)], axis=0)
    s = jnp.where(ok, s * SCALE, NEG)
    top = jnp.max(s, axis=2, keepdims=True)
    p = jnp.where(ok, jnp.exp(s - top), 0.0)
    total = jnp.sum(p, axis=2, keepdims=True)
    p = p.astype(BF)
    out = jnp.concatenate([mix(d, p[d])[None] for d in range(NEAR)], axis=0)
    write(slice(None), top, total, out)
    most = tile_ref[DEV, base]
    for d in range(1, NEAR):
        most = jnp.maximum(most, tile_ref[DEV, base + d])

    @pl.when(most > JOBS)
    def _():
        acc[...] = out
        tops[...] = jnp.broadcast_to(top, tops.shape)
        sums[...] = jnp.broadcast_to(total, sums.shape)
        for d in range(NEAR):
            num = tile_ref[DEV, base + d]

            @pl.loop(1, (num + JOBS - 1) // JOBS)
            def _(c):
                fetch(d, c * JOBS)
                wide = spread(got_ref[(base + d) * TILES + META], c * JOBS)
                ok = (wide[2:3] == want) & (tok < wide[3:4])
                s = jnp.where(ok, scores(d, got_ref[pl.ds((base + d) * TILES + 16, 2)].reshape(ROWS, HD)) * SCALE, NEG)
                best = jnp.maximum(tops[d], jnp.max(s, axis=1, keepdims=True))
                p = jnp.where(ok, jnp.exp(s - best[:, :1]), 0.0)
                old = jnp.exp(tops[d] - best)
                acc[d] = old * acc[d] + mix(d, p.astype(BF))
                sums[d] = old * sums[d] + jnp.sum(p, axis=1, keepdims=True)
                tops[d] = best

            @pl.when(num > JOBS)
            def _():
                write(d, tops[d], sums[d], acc[d])


def owner_attention(got):
    return pl.pallas_call(
        owner_kernel,
        grid=(DEV // NEAR,),
        in_specs=[pl.BlockSpec(memory_space=pltpu.VMEM)],
        out_specs=pl.BlockSpec((NEAR, ROWS, 2 * HD), lambda i: (i, 0, 0)),
        scratch_shapes=[
            pltpu.VMEM((NEAR, JOBS, TOK, HD), BF),
            pltpu.VMEM((NEAR, JOBS, TOK, HD), BF),
            pltpu.VMEM((NEAR, ROWS, HD), F32),
            pltpu.VMEM((NEAR, ROWS, HD), F32),
            pltpu.VMEM((NEAR, ROWS, HD), F32),
            pltpu.VMEM((DEV + TOK, HD), jnp.int32),
            pltpu.SMEM((DEV + TOK, HD), jnp.int32),
            pltpu.SemaphoreType.DMA,
        ],
        out_shape=jax.ShapeDtypeStruct((DEV, ROWS, 2 * HD), BF),
        cost_estimate=pl.CostEstimate(flops=4 * 2048 * 256 * 128, bytes_accessed=8_000_000, transcendentals=600_000),
                compiler_params=pltpu.CompilerParams(vmem_limit_bytes=VMEM_LIMIT),
                name="owner_attention",
    )(got)


def combine_kernel(got_ref, o_ref, m_ref, l_ref, out_ref):
    lane = lax.broadcasted_iota(jnp.int32, (HD, HD), 0)
    top_of = (lane < 3).astype(F32).astype(BF)
    sum_of = ((lane >= 3) & (lane < 5)).astype(F32).astype(BF)
    stats = got_ref[:, :, HD:].reshape(HEADS * NPG * ROWS, HD)
    tops = dot(stats, top_of).reshape(HEADS, NPG, ROWS, HD)
    sums = dot(stats, sum_of).reshape(HEADS, NPG, ROWS, HD)
    for h in range(HEADS):
        at = slice(h * HD, (h + 1) * HD)
        got = got_ref[h * NPG : (h + 1) * NPG, :, :HD].astype(F32)
        lm = m_ref[:, at]
        best = jnp.maximum(jnp.max(tops[h], axis=0), lm)
        w = jnp.exp(tops[h] - best[None])
        mine = jnp.exp(lm - best)
        mixed = jnp.sum(w * got, axis=0) + mine * o_ref[:, at]
        mixed = (mixed / (jnp.sum(w * sums[h], axis=0) + mine * l_ref[:, at])).astype(BF)
        for t in range(STEPS):
            out_ref[t, :, at] = mixed[t * RD : (t + 1) * RD]


def combine(got, o, m, l):
    vmem = pl.BlockSpec(memory_space=pltpu.VMEM)
    return pl.pallas_call(
        combine_kernel,
        in_specs=[vmem] * 4,
        out_specs=vmem,
        out_shape=jax.ShapeDtypeStruct((STEPS, RD, FEAT), BF),
        cost_estimate=pl.CostEstimate(flops=4 * 16 * 1024 * 2048, bytes_accessed=2_000_000, transcendentals=300_000),
        compiler_params=pltpu.CompilerParams(vmem_limit_bytes=VMEM_LIMIT),
        name="combine_attention",
    )(got, o, m, l)


def state_kernel(br_ref, c_ref, st_ref, out_ref):
    c = c_ref[...]
    first = dot(c, st_ref[0], NT)
    second = dot(c, st_ref[1], NT)
    which = br_ref[...]
    z = jnp.where(which == 0, first, 0.0) + jnp.where(which == 1, second, 0.0)
    out_ref[...] = z.astype(BF)


def state_products(which, c_all, states):
    wide = 1024
    return pl.pallas_call(
        state_kernel,
        grid=(MF // wide,),
        in_specs=[
            pl.BlockSpec((NPG * ROWS, 1), lambda i: (0, 0)),
            pl.BlockSpec((NPG * ROWS, ST), lambda i: (0, 0)),
            pl.BlockSpec((2, wide, ST), lambda i: (0, i, 0)),
        ],
        out_specs=pl.BlockSpec((NPG * ROWS, wide), lambda i: (0, i)),
        out_shape=jax.ShapeDtypeStruct((NPG * ROWS, MF), BF),
        cost_estimate=pl.CostEstimate(flops=4 * 128 * 128 * 4096, bytes_accessed=3_200_000, transcendentals=0),
        compiler_params=pltpu.CompilerParams(vmem_limit_bytes=VMEM_LIMIT),
        name="state_products",
    )(which, c_all, states)


def scan_kernel(coef_ref, x_ref, z_ref, out_ref):
    wide = out_ref.shape[2]
    head = lax.broadcasted_iota(jnp.int32, (MH, wide), 0)
    chan = lax.broadcasted_iota(jnp.int32, (MH, wide), 1) + pl.program_id(0) * wide
    spread = (head == chan // MD).astype(BF)
    hi, mid, lo = split3(coef_ref[...])
    coef = dot(hi, spread) + dot(mid, spread) + dot(lo, spread)
    y = coef[:ROWS] * z_ref[...].astype(F32)
    x = x_ref[...].astype(F32)
    for t in range(STEPS):
        xt = jnp.concatenate([x[t * RD : (t + 1) * RD]] * STEPS, axis=0)
        y = y + coef[(t + 1) * ROWS : (t + 2) * ROWS] * xt
    y = y.astype(BF)
    for t in range(STEPS):
        out_ref[t] = y[t * RD : (t + 1) * RD]


def scan_outputs(coef, x, z):
    wide = 1024
    spec = pl.BlockSpec((ROWS, wide), lambda i: (0, i))
    return pl.pallas_call(
        scan_kernel,
        grid=(MF // wide,),
        in_specs=[pl.BlockSpec(coef.shape, lambda i: (0, 0))] + [spec] * 2,
        out_specs=pl.BlockSpec((STEPS, RD, wide), lambda i: (0, 0, i)),
        out_shape=jax.ShapeDtypeStruct((STEPS, RD, MF), BF),
        cost_estimate=pl.CostEstimate(flops=6 * 80 * 64 * 4096, bytes_accessed=1_500_000, transcendentals=0),
        compiler_params=pltpu.CompilerParams(vmem_limit_bytes=VMEM_LIMIT),
        name="scan_outputs",
    )(coef, x, z)


def coefficients(mamba_bc, mamba_dt, decay_rate):
    delta = jax.nn.softplus(mamba_dt.astype(F32))
    rate = -decay_rate[None, :] * delta
    decay = jnp.exp(rate)
    b, c = mamba_bc[:, :, :ST], mamba_bc[:, :, ST:]
    bc = jnp.einsum("trn,srn->tsr", b, c, preferred_element_type=F32)
    rows = []
    run = decay[0]
    for s in range(STEPS):
        rows.append(run)
        if s + 1 < STEPS:
            run = run * decay[s + 1]
    zero = jnp.zeros_like(run)
    for t in range(STEPS):
        carry = delta[t]
        for s in range(STEPS):
            if s < t:
                rows.append(zero)
                continue
            if s > t:
                carry = carry * decay[s]
            rows.append(carry * bc[t, s][:, None])
    return jnp.stack(rows).reshape((1 + STEPS) * ROWS, MH)


def on_device(
    kv_store,
    local_kv,
    new_qkv,
    page_owner,
    page_slot,
    prefix_len,
    prefix_states,
    branch_id,
    mamba_x,
    mamba_bc,
    mamba_dt,
    decay_rate,
):
    my_page = lax.axis_index("page")
    q = new_qkv[:, :, 0].reshape(ROWS, FEAT)
    nk = new_qkv[:, :, 1].reshape(ROWS, FEAT)
    nv = new_qkv[:, :, 2].reshape(ROWS, FEAT)

    x_own = mamba_x.reshape(ROWS, MF)
    c_own = jnp.concatenate([mamba_bc[:, :, ST:].reshape(ROWS, ST), x_own], axis=1)
    c_all = lax.all_gather(c_own, "page", axis=0, tiled=True)
    branch = branch_id.reshape(NPG, 1, RD) - 2 * my_page
    branch = jnp.broadcast_to(branch, (NPG, STEPS, RD)).reshape(NPG * ROWS, 1)
    z = state_products(branch, c_all, prefix_states.reshape(2, MF, ST))
    z = lax.psum_scatter(z.reshape(NPG, ROWS, MF), "page", scatter_dimension=0, tiled=True)

    sent = pack(prefix_len, page_owner, page_slot, kv_store, new_qkv.transpose(0, 2, 1, 3))
    got_q = lax.all_to_all(sent.reshape(DEV, TILES, TOK, HD), ("req", "page"), 0, 0, tiled=True)

    coef = coefficients(mamba_bc, mamba_dt, decay_rate)
    mamba_out = scan_outputs(coef, x_own, z.reshape(ROWS, MF))

    o, m, l = local_attention(q, nk, nv, local_kv)

    got_q, o, m, l = lax.optimization_barrier((got_q, o, m, l))
    part = owner_attention(got_q.reshape(DEV * TILES, TOK, HD))
    got = lax.all_to_all(part, ("req", "page"), 0, 0, tiled=True)
    attn = combine(got, o, m, l)
    return attn, mamba_out


def solution(mesh):
    in_specs = (
        P(("req", "page"), None, None, None),
        P(("req", "page"), None, None, None),
        P(None, ("req", "page"), None, None),
        P(("req", "page"), None),
        P(("req", "page"), None),
        P(("req", "page")),
        P("page", None, None, None),
        P("req"),
        P(None, ("req", "page"), None),
        P(None, ("req", "page"), None),
        P(None, ("req", "page"), None),
        P(),
    )
    out_specs = (P(None, ("req", "page"), None), P(None, ("req", "page"), None))
    return jax.shard_map(
        on_device, mesh=mesh, in_specs=in_specs, out_specs=out_specs, check_vma=False
    )
```

```python
import functools
import math

import jax
import jax.numpy as jnp
from jax import lax
from jax.experimental import pallas as pl
from jax.experimental.pallas import tpu as pltpu
from jax.sharding import PartitionSpec as P

HEADS = 16
HD = 128
STEPS = 4
RD = 4
ROWS = STEPS * RD
FEAT = HEADS * HD
DEV = 128
TOK = 8
MH = 64
MD = 64
ST = 128
MF = MH * MD
NPG = 8
PAGES = 64
JOBS = 32
KEYS = JOBS * TOK
NEAR = 16
TILES = 19
META = 18
NEG = -1e30
VMEM_LIMIT = 20 * 1024 * 1024
SCALE = 1.0 / math.sqrt(HD)
BF = jnp.bfloat16
F32 = jnp.float32
NT = (((1,), (1,)), ((), ()))
NN = (((1,), (0,)), ((), ()))


def dot(a, b, dims=NN):
    return lax.dot_general(a, b, dims, preferred_element_type=F32)


def split2(x):
    hi = x.astype(BF)
    return hi, (x - hi.astype(F32)).astype(BF)


def split3(x):
    hi = x.astype(BF)
    rest = x - hi.astype(F32)
    mid = rest.astype(BF)
    return hi, mid, (rest - mid.astype(F32)).astype(BF)


def local_kernel(q_ref, nk_ref, nv_ref, kv_ref, o_ref, m_ref, l_ref):
    q = q_ref[...]
    parts = [dot(q, kv_ref[r, 0], NT) for r in range(RD)]
    row = lax.broadcasted_iota(jnp.int32, (ROWS, 1), 0)
    keep = row % RD
    new = dot(q, nk_ref[...], NT) * SCALE
    col = lax.broadcasted_iota(jnp.int32, (ROWS, ROWS), 1)
    ok = (col % RD == keep) & (col // RD <= row // RD)
    new = jnp.where(ok, new, NEG)
    mine = jnp.where(keep == 0, parts[0], NEG)
    for r in range(1, RD):
        mine = jnp.where(keep == r, parts[r], mine)
    mine = mine * SCALE
    top = jnp.maximum(jnp.max(mine, axis=1, keepdims=True), jnp.max(new, axis=1, keepdims=True))
    p = jnp.exp(mine - top)
    pn = jnp.where(ok, jnp.exp(new - top), 0.0)
    total = jnp.sum(p, axis=1, keepdims=True) + jnp.sum(pn, axis=1, keepdims=True)
    out = dot(pn.astype(BF), nv_ref[...])
    for r in range(RD):
        out = out + dot(jnp.where(keep == r, p, 0.0).astype(BF), kv_ref[r, 1])
    o_ref[...] = out
    m_ref[...] = jnp.broadcast_to(top, (ROWS, HD))
    l_ref[...] = jnp.broadcast_to(total, (ROWS, HD))


def local_attention(q, nk, nv, local_kv):
    row = pl.BlockSpec((ROWS, HD), lambda h: (0, h))
    return pl.pallas_call(
        local_kernel,
        grid=(HEADS,),
        in_specs=[row, row, row, pl.BlockSpec((RD, 2, 256, HD), lambda h: (0, 0, 0, h))],
        out_specs=[row, row, row],
        out_shape=[jax.ShapeDtypeStruct((ROWS, FEAT), F32)] * 3,
        cost_estimate=pl.CostEstimate(flops=2 * 2 * 16 * 1024 * 2048, bytes_accessed=9_000_000, transcendentals=300_000),
        compiler_params=pltpu.CompilerParams(vmem_limit_bytes=VMEM_LIMIT),
        name="local_attention",
    )(q, nk, nv, local_kv)


def pack_kernel(len_ref, own_all, slot_all, kv_ref, q_all, out_ref, buf, lists, qbuf, own_ref, slot_ref, q_ref, near, sem):
    small = []
    for i, (src, dst) in enumerate(((own_all, own_ref), (slot_all, slot_ref), (q_all, q_ref))):
        small.append(pltpu.make_async_copy(src, dst, near.at[i]))
        small[-1].start()
    copies = []
    for m in range(HEADS):
        src = kv_ref.at[:, :, :, pl.ds(m * HD, HD)]
        copies.append(pltpu.make_async_copy(src, buf.at[m, :, pl.ds(0, 16)], sem.at[0, m]))
        copies[-1].start()
    for copy in small:
        copy.wait()
    path = own_ref.shape[1]
    lane = lax.broadcasted_iota(jnp.int32, (8, HD), 1)
    row = lax.broadcasted_iota(jnp.int32, (8, HD), 0)
    owner = jnp.concatenate([own_ref[r : r + 1] for r in range(RD)], axis=1)
    slot = jnp.concatenate([slot_ref[r : r + 1] for r in range(RD)], axis=1)
    req = lane // path
    size = jnp.where(req == 0, len_ref[0], len_ref[1])
    size = jnp.where(req == 2, len_ref[2], jnp.where(req == 3, len_ref[3], size))
    count = jnp.clip(size - TOK * (lane % path), 0, TOK)
    vals = jnp.where(row == 0, owner, jnp.where(row == 1, slot % 8, 0))
    vals = jnp.where(row == 2, req + 1, jnp.where(row == 3, count, vals))
    vals = vals.astype(F32).astype(BF)
    inside = (slot // 8 == row) & (count > 0)
    up = lax.broadcasted_iota(jnp.int32, (HD, HD), 0) < lax.broadcasted_iota(jnp.int32, (HD, HD), 1)
    rank = dot(inside.astype(F32).astype(BF), up.astype(F32).astype(BF))
    rank = jnp.transpose(jnp.where(inside, rank, -1.0))
    place = lax.broadcasted_iota(jnp.int32, (HD, HD), 1).astype(F32)
    for i in range(NPG):
        mine = rank[:, i : i + 1]
        out = dot(vals, (mine == place).astype(F32).astype(BF))
        number = jnp.sum((mine >= 0).astype(F32), axis=0, keepdims=True)
        lists[i] = jnp.where(row == 4, number, out).astype(BF)
    for t in range(STEPS):
        qbuf[t * RD : (t + 1) * RD] = q_ref[t, 0].astype(F32)

    for m in range(HEADS):
        at = slice(m * HD, (m + 1) * HD)
        q = qbuf[:, at].astype(BF).reshape(1, 2, TOK, HD)
        buf[m, :, 16:18] = jnp.broadcast_to(q, (NPG, 2, TOK, HD))
        buf[m, :, META] = lists[...]
    back = []
    for m in range(HEADS):
        copies[m].wait()
        back.append(pltpu.make_async_copy(buf.at[m], out_ref.at[m], sem.at[1, m]))
        back[-1].start()
    for copy in back:
        copy.wait()


def pack(lens, owner, slot, kv_store, qkv):
    return pl.pallas_call(
        pack_kernel,
        in_specs=[pl.BlockSpec(memory_space=pltpu.SMEM)] + [pl.BlockSpec(memory_space=pl.ANY)] * 4,
        out_specs=pl.BlockSpec(memory_space=pl.ANY),
        scratch_shapes=[
            pltpu.VMEM((HEADS, NPG, TILES, TOK, HD), BF),
            pltpu.VMEM((NPG, TOK, HD), BF),
            pltpu.VMEM((ROWS, FEAT), F32),
            pltpu.VMEM(owner.shape, jnp.int32),
            pltpu.VMEM(slot.shape, jnp.int32),
            pltpu.VMEM(qkv.shape, BF),
            pltpu.SemaphoreType.DMA((3,)),
            pltpu.SemaphoreType.DMA((2, HEADS)),
        ],
        out_shape=jax.ShapeDtypeStruct((HEADS, NPG, TILES, TOK, HD), BF),
        cost_estimate=pl.CostEstimate(flops=1_000_000, bytes_accessed=10_000_000, transcendentals=0),
        name="pack",
    )(lens, owner, slot, kv_store.reshape(NPG, 16, TOK, FEAT), qkv)


def owner_kernel(all_ref, meta_ref, o_ref, kbuf, vbuf, acc, tops, sums, got_ref, lists, index, tile_ref, sem):
    step = pl.program_id(0)

    @pl.when(step == 0)
    def _():
        small = pltpu.make_async_copy(meta_ref.at[:, META], lists, sem.at[0])
        large = pltpu.make_async_copy(all_ref, got_ref, sem.at[1])
        small.start()
        large.start()
        small.wait()
        table = lists[...].astype(F32)
        index[:TOK] = jnp.transpose(table[:, 4])[:TOK].astype(jnp.int32)
        index[TOK:] = jnp.transpose(table[:, 0] * TILES + 2 * table[:, 1]).astype(jnp.int32)
        copy = pltpu.make_async_copy(index, tile_ref, sem.at[2])
        copy.start()
        copy.wait()
        large.wait()

    base = step * NEAR

    def fetch(d, at):
        d_all = base + d
        for j in range(JOBS):
            tile = tile_ref[TOK + at + j, d_all]
            kbuf[d, j] = got_ref[tile]
            vbuf[d, j] = got_ref[tile + 1]

    def spread(meta, first):
        key = lax.broadcasted_iota(jnp.int32, (HD, KEYS), 1)
        pos = lax.broadcasted_iota(jnp.int32, (HD, KEYS), 0)
        return dot(meta, (pos == first + key // TOK).astype(F32).astype(BF))

    def scores(d, q):
        return dot(q, kbuf[d].reshape(KEYS, HD), NT)

    def mix(d, p):
        return dot(p, vbuf[d].reshape(KEYS, HD))

    def write(dst, top, total, out):
        lane = lax.broadcasted_iota(jnp.int32, top.shape[:-1] + (HD,), top.ndim - 1)
        stats = jnp.zeros(lane.shape, F32)
        for i, part in enumerate(list(split3(top)) + list(split2(total))):
            stats = jnp.where(lane == i, part.astype(F32), stats)
        o_ref[dst, :, HD:] = stats.astype(BF)
        o_ref[dst, :, :HD] = out.astype(BF)

    for d in range(NEAR):
        fetch(d, 0)
    tok = (lax.broadcasted_iota(jnp.int32, (1, KEYS), 1) % TOK).astype(F32)
    want = (lax.broadcasted_iota(jnp.int32, (ROWS, 1), 0) % RD + 1).astype(F32)
    queries = [got_ref[pl.ds((base + d) * TILES + 16, 2)].reshape(ROWS, HD) for d in range(NEAR)]
    meta = jnp.concatenate([got_ref[(base + d) * TILES + META] for d in range(NEAR)], axis=0)
    wide = spread(meta, 0).reshape(NEAR, 8, KEYS)
    ok = (wide[:, 2:3] == want[None]) & (tok[None] < wide[:, 3:4])
    s = jnp.concatenate([scores(d, queries[d])[None] for d in range(NEAR)], axis=0)
    s = jnp.where(ok, s * SCALE, NEG)
    top = jnp.max(s, axis=2, keepdims=True)
    p = jnp.where(ok, jnp.exp(s - top), 0.0)
    total = jnp.sum(p, axis=2, keepdims=True)
    p = p.astype(BF)
    out = jnp.concatenate([mix(d, p[d])[None] for d in range(NEAR)], axis=0)
    write(slice(None), top, total, out)
    most = tile_ref[0, base]
    for d in range(1, NEAR):
        most = jnp.maximum(most, tile_ref[0, base + d])

    @pl.when(most > JOBS)
    def _():
        acc[...] = out
        tops[...] = jnp.broadcast_to(top, tops.shape)
        sums[...] = jnp.broadcast_to(total, sums.shape)
        for d in range(NEAR):
            num = tile_ref[0, base + d]

            @pl.loop(1, (num + JOBS - 1) // JOBS)
            def _(c):
                fetch(d, c * JOBS)
                wide = spread(got_ref[(base + d) * TILES + META], c * JOBS)
                ok = (wide[2:3] == want) & (tok < wide[3:4])
                s = jnp.where(ok, scores(d, got_ref[pl.ds((base + d) * TILES + 16, 2)].reshape(ROWS, HD)) * SCALE, NEG)
                best = jnp.maximum(tops[d], jnp.max(s, axis=1, keepdims=True))
                p = jnp.where(ok, jnp.exp(s - best[:, :1]), 0.0)
                old = jnp.exp(tops[d] - best)
                acc[d] = old * acc[d] + mix(d, p.astype(BF))
                sums[d] = old * sums[d] + jnp.sum(p, axis=1, keepdims=True)
                tops[d] = best

            @pl.when(num > JOBS)
            def _():
                write(d, tops[d], sums[d], acc[d])


def owner_attention(got):
    return pl.pallas_call(
        owner_kernel,
        grid=(DEV // NEAR,),
        in_specs=[pl.BlockSpec(memory_space=pl.ANY)] * 2,
        out_specs=pl.BlockSpec((NEAR, ROWS, 2 * HD), lambda i: (i, 0, 0)),
        scratch_shapes=[
            pltpu.VMEM((NEAR, JOBS, TOK, HD), BF),
            pltpu.VMEM((NEAR, JOBS, TOK, HD), BF),
            pltpu.VMEM((NEAR, ROWS, HD), F32),
            pltpu.VMEM((NEAR, ROWS, HD), F32),
            pltpu.VMEM((NEAR, ROWS, HD), F32),
            pltpu.VMEM((DEV * TILES, TOK, HD), BF),
            pltpu.VMEM((DEV, TOK, HD), BF),
            pltpu.VMEM((DEV + TOK, HD), jnp.int32),
            pltpu.SMEM((DEV + TOK, HD), jnp.int32),
            pltpu.SemaphoreType.DMA((3,)),
        ],
        out_shape=jax.ShapeDtypeStruct((DEV, ROWS, 2 * HD), BF),
        cost_estimate=pl.CostEstimate(flops=4 * 2048 * 256 * 128, bytes_accessed=8_000_000, transcendentals=600_000),
                        name="owner_attention",
    )(got.reshape(DEV * TILES, TOK, HD), got)


def combine_kernel(got_ref, o_ref, m_ref, l_ref, out_ref):
    lane = lax.broadcasted_iota(jnp.int32, (HD, HD), 0)
    top_of = (lane < 3).astype(F32).astype(BF)
    sum_of = ((lane >= 3) & (lane < 5)).astype(F32).astype(BF)
    stats = got_ref[:, :, HD:].reshape(HEADS * NPG * ROWS, HD)
    tops = dot(stats, top_of).reshape(HEADS, NPG, ROWS, HD)
    sums = dot(stats, sum_of).reshape(HEADS, NPG, ROWS, HD)
    for h in range(HEADS):
        at = slice(h * HD, (h + 1) * HD)
        got = got_ref[h * NPG : (h + 1) * NPG, :, :HD].astype(F32)
        lm = m_ref[:, at]
        best = jnp.maximum(jnp.max(tops[h], axis=0), lm)
        w = jnp.exp(tops[h] - best[None])
        mine = jnp.exp(lm - best)
        mixed = jnp.sum(w * got, axis=0) + mine * o_ref[:, at]
        mixed = (mixed / (jnp.sum(w * sums[h], axis=0) + mine * l_ref[:, at])).astype(BF)
        for t in range(STEPS):
            out_ref[t, :, at] = mixed[t * RD : (t + 1) * RD]


def combine(got, o, m, l):
    vmem = pl.BlockSpec(memory_space=pltpu.VMEM)
    return pl.pallas_call(
        combine_kernel,
        in_specs=[vmem] * 4,
        out_specs=vmem,
        out_shape=jax.ShapeDtypeStruct((STEPS, RD, FEAT), BF),
        cost_estimate=pl.CostEstimate(flops=4 * 16 * 1024 * 2048, bytes_accessed=2_000_000, transcendentals=300_000),
        compiler_params=pltpu.CompilerParams(vmem_limit_bytes=VMEM_LIMIT),
        name="combine_attention",
    )(got, o, m, l)


def state_kernel(br_ref, c_ref, st_ref, out_ref):
    c = c_ref[...]
    first = dot(c, st_ref[0], NT)
    second = dot(c, st_ref[1], NT)
    which = br_ref[...]
    z = jnp.where(which == 0, first, 0.0) + jnp.where(which == 1, second, 0.0)
    out_ref[...] = z.astype(BF)


def state_products(which, c_all, states):
    wide = 1024
    return pl.pallas_call(
        state_kernel,
        grid=(MF // wide,),
        in_specs=[
            pl.BlockSpec((NPG * ROWS, 1), lambda i: (0, 0)),
            pl.BlockSpec((NPG * ROWS, ST), lambda i: (0, 0)),
            pl.BlockSpec((2, wide, ST), lambda i: (0, i, 0)),
        ],
        out_specs=pl.BlockSpec((NPG * ROWS, wide), lambda i: (0, i)),
        out_shape=jax.ShapeDtypeStruct((NPG * ROWS, MF), BF),
        cost_estimate=pl.CostEstimate(flops=4 * 128 * 128 * 4096, bytes_accessed=3_200_000, transcendentals=0),
        compiler_params=pltpu.CompilerParams(vmem_limit_bytes=VMEM_LIMIT),
        name="state_products",
    )(which, c_all, states)


def scan_kernel(coef_ref, x_ref, z_ref, out_ref):
    wide = out_ref.shape[2]
    head = lax.broadcasted_iota(jnp.int32, (MH, wide), 0)
    chan = lax.broadcasted_iota(jnp.int32, (MH, wide), 1) + pl.program_id(0) * wide
    spread = (head == chan // MD).astype(BF)
    hi, mid, lo = split3(coef_ref[...])
    coef = dot(hi, spread) + dot(mid, spread) + dot(lo, spread)
    y = coef[:ROWS] * z_ref[...].astype(F32)
    x = x_ref[...].astype(F32)
    for t in range(STEPS):
        xt = jnp.concatenate([x[t * RD : (t + 1) * RD]] * STEPS, axis=0)
        y = y + coef[(t + 1) * ROWS : (t + 2) * ROWS] * xt
    y = y.astype(BF)
    for t in range(STEPS):
        out_ref[t] = y[t * RD : (t + 1) * RD]


def scan_outputs(coef, x, z):
    wide = 1024
    spec = pl.BlockSpec((ROWS, wide), lambda i: (0, i))
    return pl.pallas_call(
        scan_kernel,
        grid=(MF // wide,),
        in_specs=[pl.BlockSpec(coef.shape, lambda i: (0, 0))] + [spec] * 2,
        out_specs=pl.BlockSpec((STEPS, RD, wide), lambda i: (0, 0, i)),
        out_shape=jax.ShapeDtypeStruct((STEPS, RD, MF), BF),
        cost_estimate=pl.CostEstimate(flops=6 * 80 * 64 * 4096, bytes_accessed=1_500_000, transcendentals=0),
        compiler_params=pltpu.CompilerParams(vmem_limit_bytes=VMEM_LIMIT),
        name="scan_outputs",
    )(coef, x, z)


def coefficients(mamba_bc, mamba_dt, decay_rate):
    delta = jax.nn.softplus(mamba_dt.astype(F32))
    rate = -decay_rate[None, :] * delta
    decay = jnp.exp(rate)
    b, c = mamba_bc[:, :, :ST], mamba_bc[:, :, ST:]
    bc = jnp.einsum("trn,srn->tsr", b, c, preferred_element_type=F32)
    rows = []
    run = decay[0]
    for s in range(STEPS):
        rows.append(run)
        if s + 1 < STEPS:
            run = run * decay[s + 1]
    zero = jnp.zeros_like(run)
    for t in range(STEPS):
        carry = delta[t]
        for s in range(STEPS):
            if s < t:
                rows.append(zero)
                continue
            if s > t:
                carry = carry * decay[s]
            rows.append(carry * bc[t, s][:, None])
    return jnp.stack(rows).reshape((1 + STEPS) * ROWS, MH)


def on_device(
    kv_store,
    local_kv,
    new_qkv,
    page_owner,
    page_slot,
    prefix_len,
    prefix_states,
    branch_id,
    mamba_x,
    mamba_bc,
    mamba_dt,
    decay_rate,
):
    my_page = lax.axis_index("page")
    q = new_qkv[:, :, 0].reshape(ROWS, FEAT)
    nk = new_qkv[:, :, 1].reshape(ROWS, FEAT)
    nv = new_qkv[:, :, 2].reshape(ROWS, FEAT)

    x_own = mamba_x.reshape(ROWS, MF)
    c_own = jnp.concatenate([mamba_bc[:, :, ST:].reshape(ROWS, ST), x_own], axis=1)
    c_all = lax.all_gather(c_own, "page", axis=0, tiled=True)
    branch = branch_id.reshape(NPG, 1, RD) - 2 * my_page
    branch = jnp.broadcast_to(branch, (NPG, STEPS, RD)).reshape(NPG * ROWS, 1)
    z = state_products(branch, c_all, prefix_states.reshape(2, MF, ST))
    z = lax.psum_scatter(z.reshape(NPG, ROWS, MF), "page", scatter_dimension=0, tiled=True)

    sent = pack(prefix_len, page_owner, page_slot, kv_store, new_qkv.transpose(0, 2, 1, 3))
    got_q = lax.all_to_all(sent.reshape(DEV, TILES, TOK, HD), ("req", "page"), 0, 0, tiled=True)

    coef = coefficients(mamba_bc, mamba_dt, decay_rate)
    mamba_out = scan_outputs(coef, x_own, z.reshape(ROWS, MF))

    o, m, l = local_attention(q, nk, nv, local_kv)

    got_q, o, m, l = lax.optimization_barrier((got_q, o, m, l))
    part = owner_attention(got_q)
    got = lax.all_to_all(part, ("req", "page"), 0, 0, tiled=True)
    attn = combine(got, o, m, l)
    return attn, mamba_out


def solution(mesh):
    in_specs = (
        P(("req", "page"), None, None, None),
        P(("req", "page"), None, None, None),
        P(None, ("req", "page"), None, None),
        P(("req", "page"), None),
        P(("req", "page"), None),
        P(("req", "page")),
        P("page", None, None, None),
        P("req"),
        P(None, ("req", "page"), None),
        P(None, ("req", "page"), None),
        P(None, ("req", "page"), None),
        P(),
    )
    out_specs = (P(None, ("req", "page"), None), P(None, ("req", "page"), None))
    return jax.shard_map(
        on_device, mesh=mesh, in_specs=in_specs, out_specs=out_specs, check_vma=False
    )
```
